256 devices in a mesh: col: 32 (over x_hi, z, core), row: 8 (over x_lo, y).
Axes of the slice: x: 4 (x_hi: 2, x_lo: 2; x = x_hi * 2 + x_lo), y: 4, z: 8, core: 2. Of those that a mesh axis runs over, the one named last changes fastest.
Arguments:
- matrix: float32 [64, 64, 128, 128], P('col', 'row'), may hold values from -12 to 80, as said below
- col_owner: int32 [64], replicated, may hold values from 0 to 63, as said below
- row_owner: int32 [64], replicated, may hold values from 0 to 63, as said below
- pattern: int32 [2, 64], replicated, may hold values from 0 to 1, as said below
Outputs:
- factored: float32 [64, 64, 128, 128], P('col', 'row')
The draws below stay inside these ranges and needn't reach their ends.
Inputs may be any that keep to these rules, and one draw needn't show every extreme that they name: `col_owner`: a permutation of 0 to 63. `row_owner`: a permutation of 0 to 63. pattern[0, 1] is 1; pattern[k, i] is 0 for i <= k; pattern[1, i] >= pattern[0, i] for every i >= 2. `matrix`: the diagonal tile of every supernode is symmetric positive definite, and so is every diagonal tile after the updates.
All inputs are finite; a program needn't handle non-finite values.
Results may differ from the reference program's by a relative error of at most 0.0003.
Values sent between devices are 32-bit elements; how exact they have to be, the bound alone decides.
A program may use at most 64 MiB of HBM per device.

```python
import jax
import jax.numpy as jnp
from jax import lax

WIDTH = 128
NODES = 64


def owner_maps(key):
    col_map = jax.random.permutation(jax.random.fold_in(key, 11), NODES).astype(jnp.int32)
    row_map = jax.random.permutation(jax.random.fold_in(key, 13), NODES).astype(jnp.int32)
    return (col_map, row_map)


def draw_col_owner(key, part):
    return owner_maps(key)[0]


def draw_row_owner(key, part):
    return owner_maps(key)[1]


def draw_pattern(key, part):
    ordinal = jnp.arange(NODES, dtype=jnp.int32)
    first_rows = jax.random.randint(jax.random.fold_in(key, 17), (NODES,), 0, 2).astype(jnp.int32)
    extra_rows = (jax.random.randint(jax.random.fold_in(key, 19), (NODES,), 0, 4) == 0).astype(jnp.int32)
    first_rows = jnp.where(ordinal == 1, 1, jnp.where(ordinal < 1, 0, first_rows)).astype(jnp.int32)
    second_rows = jnp.where(ordinal <= 1, 0, jnp.maximum(first_rows, extra_rows)).astype(jnp.int32)
    return jnp.stack([first_rows, second_rows]).astype(jnp.int32)


def draw_matrix(key, part):
    col_map, row_map = owner_maps(key)
    full_shape = (NODES, NODES, WIDTH, WIDTH)
    base_noise = jax.random.normal(jax.random.fold_in(key, 23), full_shape, jnp.float32)
    diag_mark = jnp.zeros((NODES, NODES), jnp.float32).at[col_map, row_map].set(1.0)
    symmetric = (base_noise + jnp.swapaxes(base_noise, 2, 3)) * 0.85
    diag_lift = jax.random.uniform(jax.random.fold_in(key, 29), (NODES, NODES, WIDTH), jnp.float32, 56.0, 72.0)
    identity = jnp.eye(WIDTH, dtype=jnp.float32)
    diag_tiles = symmetric + diag_lift[..., None] * identity
    return jnp.where(diag_mark[:, :, None, None] > 0.5, diag_tiles, base_noise).astype(jnp.float32)


def setup_inputs(seed: int = 0) -> dict:
    arg_keys = jax.random.split(jax.random.key(seed), 5)
    matrix = draw_matrix(jax.random.fold_in(arg_keys[4], 71), 0)
    col_owner = draw_col_owner(jax.random.fold_in(arg_keys[4], 71), 0)
    row_owner = draw_row_owner(jax.random.fold_in(arg_keys[4], 71), 0)
    pattern = draw_pattern(jax.random.fold_in(arg_keys[4], 71), 0)
    return {"matrix": matrix, "col_owner": col_owner, "row_owner": row_owner, "pattern": pattern}


PRECISE = lax.Precision.HIGHEST

def panel_factors(column, diag_tile, kept_rows):
    lower_tri = jnp.linalg.cholesky(diag_tile)
    identity = jnp.eye(lower_tri.shape[0], dtype=lower_tri.dtype)
    inverse = lax.linalg.triangular_solve(lower_tri, identity, left_side=True, lower=True)
    scaled = jnp.einsum('spq,rq->spr', column, inverse, precision=PRECISE)
    return (lower_tri, jnp.where(kept_rows[:, None, None], scaled, jnp.zeros_like(scaled)))

def reference(matrix, col_owner, row_owner, pattern):
    node_count = matrix.shape[0]
    ordinal = jnp.arange(node_count, dtype=jnp.int32)
    col_node = jnp.zeros((node_count,), jnp.int32).at[col_owner].set(ordinal)
    row_node = jnp.zeros((node_count,), jnp.int32).at[row_owner].set(ordinal)
    for panel_id in range(2):
        position = col_owner[panel_id]
        column = matrix[position]
        diag_tile = column[row_owner[panel_id]]
        kept_rows = pattern[panel_id][row_node] == 1
        lower_tri, row_factors = panel_factors(column, diag_tile, kept_rows)
        col_factors = row_factors[row_owner[col_node]]

        def update(operands):
            column_tiles, factor, col_id = operands
            lower_half = row_node >= col_id
            product = jnp.einsum('spq,rq->spr', row_factors, factor, precision=PRECISE)
            return column_tiles - jnp.where(lower_half[:, None, None], product, jnp.zeros_like(product))
        matrix = lax.map(update, (matrix, col_factors, col_node))
        old_column = matrix[position]
        is_diag = row_node == panel_id
        new_column = jnp.where(is_diag[:, None, None], lower_tri[None], jnp.where(kept_rows[:, None, None], row_factors, old_column))
        matrix = matrix.at[position].set(new_column)
    return matrix
```

```python
import functools

import jax
import jax.numpy as jnp
from jax import lax
from jax.experimental import pallas as pl
from jax.experimental.pallas import tpu as pltpu
from jax.sharding import PartitionSpec as P

MESH = pl.DeviceIdType.MESH
F32 = jnp.float32
PRECISE = lax.Precision.HIGHEST
W = 128
NODES = 64


def my_place():
    col = lax.axis_index("col")
    row = lax.axis_index("row")
    return col // 16, (col // 2) % 8, col % 2, row // 4, row % 4


def device(xh, z, k, xl, y):
    return {"col": (xh * 8 + z) * 2 + k, "row": xl * 4 + y}


def send_all(count, me, source, slot, target, send_sem, recv_sem):
    def step(q, carry):
        @pl.when(q != me)
        def _():
            pltpu.make_async_remote_copy(
                src_ref=source(q),
                dst_ref=slot(me),
                send_sem=send_sem.at[q],
                recv_sem=recv_sem.at[me],
                device_id=target(q),
                device_id_type=MESH,
            ).start()

        return carry

    lax.fori_loop(0, count, step, 0)


def recv_all(count, me, source, slot, target, send_sem, recv_sem):
    def step(q, carry):
        @pl.when(q != me)
        def _():
            copy = pltpu.make_async_remote_copy(
                src_ref=source(q),
                dst_ref=slot(q),
                send_sem=send_sem.at[q],
                recv_sem=recv_sem.at[q],
                device_id=target(q),
                device_id_type=MESH,
            )
            copy.wait_send()
            copy.wait_recv()

        return carry

    lax.fori_loop(0, count, step, 0)


def comm_kernel(
    mat, co, ro, rows_out, cols_out, diag_out,
    st1, rc1, half, rc2, pc2, rows, cst, rc3, pc3, cols,
    dst1, rd1, pd1, rd2, pd2, diag,
    s1, r1, s2, r2, s4, r4, s5, r5, s6, r6, s7, r7, d1, e1, d2, e2, d3, e3,
):
    xh, z, k, xl, y = my_place()
    me_plane = (xh * 2 + xl) * 4 + y
    me_zk = z * 2 + k
    me_xz = xh * 8 + z
    me_row = xl * 4 + y

    def plane(q):
        return device(q // 8, z, k, (q // 4) % 2, q % 4)

    def along(q):
        return device(xh, q // 2, q % 2, xl, y)

    def group(q):
        return device(q // 8, q % 8, k, xl, y)

    def row_of(q):
        return device(xh, z, k, q // 4, q % 4)

    owner = [co[p] // 2 for p in range(2)]
    local = [co[p] % 2 for p in range(2)]
    o_xh = [o // 16 for o in owner]
    o_z = [(o // 2) % 8 for o in owner]
    o_k = [o % 2 for o in owner]

    barrier = pltpu.get_barrier_semaphore()

    def greet(count, skip, target):
        def step(q, carry):
            @pl.when(jnp.logical_not(skip(q)))
            def _():
                pl.semaphore_signal(barrier, inc=1, device_id=target(q), device_id_type=MESH)

            return carry

        lax.fori_loop(0, count, step, 0)

    greet(16, lambda q: q == me_plane, plane)
    greet(16, lambda q: q == me_zk, along)
    greet(8, lambda q: q == z, lambda q: device(1 - xh, q, k, xl, y))
    pl.semaphore_wait(barrier, 37)

    lead = ((0, 0), (0, 1), (1, 1))
    for t, (p, n) in enumerate(lead):
        tile = mat[local[p], ro[n] % 8]
        for q in range(16):
            dst1[q, t] = tile[8 * q : 8 * q + 8, :]
    rd1[me_plane] = dst1[me_plane]
    d1_args = (16, me_plane, lambda q: dst1.at[q], lambda q: rd1.at[q], plane, d1, e1)
    send_all(*d1_args)

    for p in range(2):
        st1[p] = mat[local[p], pl.ds(4 * (1 - k), 4)]
    sib = device(xh, z, 1 - k, xl, y)
    split = pltpu.make_async_remote_copy(
        src_ref=st1, dst_ref=rc1, send_sem=s1, recv_sem=r1, device_id=sib, device_id_type=MESH
    )
    split.start()

    recv_all(*d1_args)
    for t, (p, n) in enumerate(lead):
        slot = ro[n] // 8
        pd1[t] = rd1[(o_xh[p] * 2 + slot // 4) * 4 + slot % 4, t]
    rd2[me_zk] = pd1[...]
    d2_args = (16, me_zk, lambda q: pd1, lambda q: rd2.at[q], along, d2, e2)
    send_all(*d2_args)
    split.wait()
    for p in range(2):
        mine = mat[local[p], pl.ds(4 * k, 4)]
        half[pl.ds(4 * p, 4)] = jnp.where(o_k[p] == k, mine, rc1[p])
    recv_all(*d2_args)
    for t, (p, n) in enumerate(lead):
        pd2[t] = rd2[o_z[p] * 2 + o_k[p], t]
    diag[me_plane] = pd2[...]
    d3_args = (16, me_plane, lambda q: pd2, lambda q: diag.at[q], plane, d3, e3)
    send_all(*d3_args)

    rc2[me_xz] = half[z, pl.ds(64 * xh, 64), :]
    r2_args = (
        16, me_xz, lambda q: half.at[q % 8, pl.ds(64 * (q // 8), 64), :],
        lambda q: rc2.at[q], group, s2, r2,
    )
    send_all(*r2_args)
    recv_all(*d3_args)
    recv_all(*r2_args)
    src = jnp.where(z < 4, o_xh[0] * 8 + o_z[0], o_xh[1] * 8 + o_z[1])
    piece = rc2[src]
    pc2[...] = piece

    def rows_slot(q):
        zz = q % 8
        return rows.at[zz // 4, 4 * k + zz % 4, pl.ds(64 * (q // 8), 64), :]

    rows[z // 4, 4 * k + z % 4, pl.ds(64 * xh, 64), :] = piece
    r4_args = (16, me_xz, lambda q: pc2, rows_slot, group, s4, r4)
    send_all(*r4_args)
    base = 2 * ((xh * 8 + z) * 2 + k)

    def find(n, carry):
        c = co[n]
        s = ro[n]
        return (
            carry[0] + jnp.where(c == base, s, 0),
            carry[1] + jnp.where(c == base + 1, s, 0),
        )

    slots = lax.fori_loop(0, NODES, find, (jnp.int32(0), jnp.int32(0)))
    recv_all(*r4_args)

    def join(p):
        mine = rows.at[p, pl.ds(4 * k, 4)]
        return pltpu.make_async_remote_copy(
            src_ref=mine, dst_ref=mine, send_sem=s5.at[p], recv_sem=r5.at[p],
            device_id=sib, device_id_type=MESH,
        )

    def joined(p):
        return pltpu.make_async_remote_copy(
            src_ref=rows.at[p, pl.ds(4 * k, 4)],
            dst_ref=rows.at[p, pl.ds(4 * (1 - k), 4)],
            send_sem=s5.at[p], recv_sem=r5.at[p], device_id=sib, device_id_type=MESH,
        )

    for p in range(2):
        join(p).start()
    for p in range(2):
        copy = joined(p)
        copy.wait_send()
        copy.wait_recv()

    for p in range(2):
        for l in range(2):
            tile = rows[p, slots[l] % 8]
            cst[4 * p + 2 * l] = tile[:64]
            cst[4 * p + 2 * l + 1] = tile[64:]
    rc3[me_row] = cst[me_row]
    c1_args = (8, me_row, lambda q: cst.at[q], lambda q: rc3.at[q], row_of, s6, r6)
    send_all(*c1_args)
    recv_all(*c1_args)
    from_row = jnp.where((me_row // 2) % 2 == 0, slots[0] // 8, slots[1] // 8)
    piece = rc3[from_row]
    pc3[...] = piece
    cols[me_row] = piece
    c2_args = (8, me_row, lambda q: pc3, lambda q: cols.at[q], row_of, s7, r7)
    send_all(*c2_args)
    recv_all(*c2_args)

    rows_out[...] = rows[...]
    cols_out[...] = cols[...]
    diag_out[...] = diag[...]


def gather_tiles(mat, co, ro):
    vmem = pl.BlockSpec(memory_space=pltpu.VMEM)
    smem = pl.BlockSpec(memory_space=pltpu.SMEM)
    dma = pltpu.SemaphoreType.DMA
    return pl.pallas_call(
        comm_kernel,
        out_shape=(
            jax.ShapeDtypeStruct((2, 8, W, W), F32),
            jax.ShapeDtypeStruct((8, 64, W), F32),
            jax.ShapeDtypeStruct((16, 3, 8, W), F32),
        ),
        in_specs=[vmem, smem, smem],
        out_specs=(vmem, vmem, vmem),
        scratch_shapes=[
            pltpu.VMEM((2, 4, W, W), F32),
            pltpu.VMEM((2, 4, W, W), F32),
            pltpu.VMEM((8, W, W), F32),
            pltpu.VMEM((16, 64, W), F32),
            pltpu.VMEM((64, W), F32),
            pltpu.VMEM((2, 8, W, W), F32),
            pltpu.VMEM((8, 64, W), F32),
            pltpu.VMEM((8, 64, W), F32),
            pltpu.VMEM((64, W), F32),
            pltpu.VMEM((8, 64, W), F32),
            pltpu.VMEM((16, 3, 8, W), F32),
            pltpu.VMEM((16, 3, 8, W), F32),
            pltpu.VMEM((3, 8, W), F32),
            pltpu.VMEM((16, 3, 8, W), F32),
            pltpu.VMEM((3, 8, W), F32),
            pltpu.VMEM((16, 3, 8, W), F32),
            dma, dma,
            dma((16,)), dma((16,)),
            dma((16,)), dma((16,)),
            dma((2,)), dma((2,)),
            dma((8,)), dma((8,)),
            dma((8,)), dma((8,)),
            dma((16,)), dma((16,)),
            dma((16,)), dma((16,)),
            dma((16,)), dma((16,)),
        ],
        compiler_params=pltpu.CompilerParams(
            collective_id=0, has_side_effects=True, vmem_limit_bytes=32 * 1024 * 1024
        ),
        name="gather_tiles",
    )(mat, co, ro)


def lanes(x):
    return jnp.broadcast_to(x, (x.shape[0], W))


def subs(x):
    return jnp.broadcast_to(x, (8, W))


def factor(wa_ref, wb_ref):
    rid = lax.broadcasted_iota(jnp.int32, (8, W), 0)
    for c in range(0, W, 8):
        wa = wa_ref[c : c + 8, :]
        wb = wb_ref[c : c + 8, :]
        cl = [lanes(wa[:, c + i : c + i + 1]) for i in range(8)]
        pa, pb, sc, lt = [], [], [], []
        for i in range(8):
            s = lax.rsqrt(subs(cl[i][i : i + 1]))
            li = cl[i] * s
            ra = subs(wa[i : i + 1]) * s
            rb = subs(wb[i : i + 1]) * s
            low = jnp.where(rid > i, li, 0.0)
            wa = jnp.where(rid == i, ra, wa - low * ra)
            wb = jnp.where(rid == i, rb, wb - low * rb)
            row = {}
            for j in range(i + 1, 8):
                row[j] = subs(li[j : j + 1])
                cl[j] = cl[j] - li * row[j]
            pa.append(ra)
            pb.append(rb)
            sc.append(s)
            lt.append(row)
        wa_ref[c : c + 8, :] = wa
        wb_ref[c : c + 8, :] = wb
        g = c + 8
        while g < W:
            size = min(16, W - g)
            tile = lambda v: jnp.concatenate([v] * (size // 8), axis=0) if size > 8 else v
            ga = wa_ref[g : g + size, :]
            gb = wb_ref[g : g + size, :]
            gc = [lanes(ga[:, c + i : c + i + 1]) for i in range(8)]
            for i in range(8):
                li = gc[i] * tile(sc[i])
                ga = ga - li * tile(pa[i])
                gb = gb - li * tile(pb[i])
                for j in range(i + 1, 8):
                    gc[j] = gc[j] - li * tile(lt[i][j])
            wa_ref[g : g + size, :] = ga
            wb_ref[g : g + size, :] = gb
            g += size


def nt(a, b):
    return lax.dot_general(a, b, (((1,), (1,)), ((), ())), precision=PRECISE, preferred_element_type=F32)


def apply_kernel(mat, rows, cols, diag, co, ro, pat, out, wa, wb, f0, f1, g0, g1, inv_row, inv_col):
    col = lax.axis_index("col")
    row = lax.axis_index("row")

    def invert(n, carry):
        inv_row[ro[n]] = n
        inv_col[co[n]] = n
        return carry

    lax.fori_loop(0, NODES, invert, 0)
    row_node = [inv_row[8 * row + s] for s in range(8)]
    col_node = [inv_col[2 * col + l] for l in range(2)]
    rid = lax.broadcasted_iota(jnp.int32, (W, W), 0)
    cid = lax.broadcasted_iota(jnp.int32, (W, W), 1)
    eye = jnp.where(rid == cid, 1.0, 0.0).astype(F32)

    def lead(t):
        return jnp.concatenate([diag[q, t] for q in range(16)], axis=0)

    def col_tile(p, l):
        return jnp.concatenate([cols[4 * p + 2 * l], cols[4 * p + 2 * l + 1]], axis=0)

    def finish(l, s, value):
        out[l, s] = value

    wa[...] = lead(0)
    wb[...] = eye
    factor(wa, wb)
    lower0 = jnp.where(rid <= cid, wa[...], 0.0).T
    inv0 = wb[...]
    f01 = nt(lead(1), inv0)
    a11 = lead(2) - nt(f01, f01)
    for s in range(8):
        keep = pat[0, row_node[s]] == 1
        f0[s] = jnp.where(keep, nt(rows[0, s], inv0), 0.0)
    for l in range(2):
        keep = pat[0, col_node[l]] == 1
        g0[l] = jnp.where(keep, nt(col_tile(0, l), inv0), 0.0)
    wa[...] = a11
    wb[...] = eye
    factor(wa, wb)
    lower1 = jnp.where(rid <= cid, wa[...], 0.0).T
    inv1 = wb[...]
    for s in range(8):
        keep = pat[1, row_node[s]] == 1
        f1[s] = jnp.where(keep, nt(rows[1, s] - nt(f0[s], f01), inv1), 0.0)
    for l in range(2):
        keep = pat[1, col_node[l]] == 1
        g1[l] = jnp.where(keep, nt(col_tile(1, l) - nt(g0[l], f01), inv1), 0.0)
    for l in range(2):
        for s in range(8):
            old = mat[l, s]
            new = old - nt(f0[s], g0[l]) - nt(f1[s], g1[l])
            new = jnp.where(row_node[s] >= col_node[l], new, old)
            for p, (f, low) in enumerate(((f0, lower0), (f1, lower1))):
                here = col_node[l] == p
                new = jnp.where(here & (pat[p, row_node[s]] == 1), f[s], new)
                new = jnp.where(here & (row_node[s] == p), low, new)
            out[l, s] = new


def apply_panels(mat, rows, cols, diag, co, ro, pat):
    vmem = pl.BlockSpec(memory_space=pltpu.VMEM)
    smem = pl.BlockSpec(memory_space=pltpu.SMEM)
    return pl.pallas_call(
        apply_kernel,
        out_shape=jax.ShapeDtypeStruct((2, 8, W, W), F32),
        in_specs=[vmem] * 4 + [smem] * 3,
        out_specs=vmem,
        scratch_shapes=[
            pltpu.VMEM((W, W), F32),
            pltpu.VMEM((W, W), F32),
            pltpu.VMEM((8, W, W), F32),
            pltpu.VMEM((8, W, W), F32),
            pltpu.VMEM((2, W, W), F32),
            pltpu.VMEM((2, W, W), F32),
            pltpu.SMEM((NODES,), jnp.int32),
            pltpu.SMEM((NODES,), jnp.int32),
        ],
        compiler_params=pltpu.CompilerParams(vmem_limit_bytes=32 * 1024 * 1024),
        name="apply_panels",
    )(mat, rows, cols, diag, co, ro, pat)


def body(matrix, col_owner, row_owner, pattern):
    rows, cols, diag = gather_tiles(matrix, col_owner, row_owner)
    return apply_panels(matrix, rows, cols, diag, col_owner, row_owner, pattern)


def solution(mesh):
    return jax.shard_map(
        body,
        mesh=mesh,
        in_specs=(P("col", "row", None, None), P(), P(), P()),
        out_specs=P("col", "row", None, None),
        check_vma=False,
    )
```

```python
import functools

import jax
import jax.numpy as jnp
from jax import lax
from jax.experimental import pallas as pl
from jax.experimental.pallas import tpu as pltpu
from jax.sharding import PartitionSpec as P

MESH = pl.DeviceIdType.MESH
F32 = jnp.float32
PRECISE = lax.Precision.HIGHEST
W = 128
NODES = 64


def my_place():
    col = lax.axis_index("col")
    row = lax.axis_index("row")
    return col // 16, (col // 2) % 8, col % 2, row // 4, row % 4


def device(xh, z, k, xl, y):
    return {"col": (xh * 8 + z) * 2 + k, "row": xl * 4 + y}


def send_all(count, me, source, slot, target, send_sem, recv_sem):
    def step(q, carry):
        @pl.when(q != me)
        def _():
            pltpu.make_async_remote_copy(
                src_ref=source(q),
                dst_ref=slot(me),
                send_sem=send_sem.at[q],
                recv_sem=recv_sem.at[me],
                device_id=target(q),
                device_id_type=MESH,
            ).start()

        return carry

    lax.fori_loop(0, count, step, 0)


def recv_all(count, me, source, slot, target, send_sem, recv_sem):
    def step(q, carry):
        @pl.when(q != me)
        def _():
            copy = pltpu.make_async_remote_copy(
                src_ref=source(q),
                dst_ref=slot(q),
                send_sem=send_sem.at[q],
                recv_sem=recv_sem.at[q],
                device_id=target(q),
                device_id_type=MESH,
            )
            copy.wait_send()
            copy.wait_recv()

        return carry

    lax.fori_loop(0, count, step, 0)


def place_lead(diag, t, dst):
    for k in range(2):
        for q in range(16):
            dst[64 * k + 4 * q : 64 * k + 4 * q + 4, :] = diag[k, q, t]


def comm_kernel(
    mat_hbm, co_hbm, ro_hbm, rows_out, cols_out, inv_out, low_out, f01_out,
    mat, co, ro, st1, rc1, stl, rcl, half, leadh, rc2, pc2, rows, cst, rc3, pc3, cols,
    dst1, rd1, pd1, rd2, diag, wa, wb, tile_a,
    ld, s1, r1, s2, r2, s4, r4, s5, r5, s6, r6, s7, r7, d1, e1, d2, e2, d3, e3, d4, e4,
):
    xh, z, k, xl, y = my_place()
    me_plane = (xh * 2 + xl) * 4 + y
    me_xz = xh * 8 + z
    me_row = xl * 4 + y

    def plane(q):
        return device(q // 8, z, k, (q // 4) % 2, q % 4)

    def along(q):
        return device(xh, q, k, xl, y)

    def group(q):
        return device(q // 8, q % 8, k, xl, y)

    def row_of(q):
        return device(xh, z, k, q // 4, q % 4)

    sib = device(xh, z, 1 - k, xl, y)
    loads = [
        pltpu.make_async_copy(co_hbm, co, ld.at[0]),
        pltpu.make_async_copy(ro_hbm, ro, ld.at[1]),
        pltpu.make_async_copy(mat_hbm, mat, ld.at[2]),
    ]
    for copy in loads:
        copy.start()

    barrier = pltpu.get_barrier_semaphore()

    def greet(count, me, target):
        def step(q, carry):
            @pl.when(q != me)
            def _():
                pl.semaphore_signal(barrier, inc=1, device_id=target(q), device_id_type=MESH)

            return carry

        lax.fori_loop(0, count, step, 0)

    greet(16, me_xz, group)
    greet(8, me_row, row_of)

    def far(q, carry):
        @pl.when(q != me_row)
        def _():
            pl.semaphore_signal(
                barrier, inc=1, device_id=device(1 - xh, z, k, q // 4, q % 4), device_id_type=MESH
            )

        return carry

    lax.fori_loop(0, 8, far, 0)
    pl.semaphore_signal(barrier, inc=1, device_id=sib, device_id_type=MESH)
    for copy in loads:
        copy.wait()

    owner = [co[p] // 2 for p in range(2)]
    local = [co[p] % 2 for p in range(2)]
    o_xh = [o // 16 for o in owner]
    o_z = [(o // 2) % 8 for o in owner]
    o_k = [o % 2 for o in owner]
    lead = ((0, 0), (0, 1), (1, 1))
    for p in range(2):
        st1[p] = mat[local[p], pl.ds(4 * (1 - k), 4)]
    for t, (p, n) in enumerate(lead):
        stl[t] = mat[local[p], ro[n] % 8, pl.ds(64 * (1 - k), 64), :]
    pl.semaphore_wait(barrier, 15 + 7 + 7 + 1)

    def to_sibling(src, dst, send, recv):
        return pltpu.make_async_remote_copy(
            src_ref=src, dst_ref=dst, send_sem=send, recv_sem=recv, device_id=sib, device_id_type=MESH
        )

    split_lead = to_sibling(stl, rcl, s1.at[0], r1.at[0])
    split_half = to_sibling(st1, rc1, s1.at[1], r1.at[1])
    split_lead.start()
    split_half.start()
    split_lead.wait()
    for t, (p, n) in enumerate(lead):
        mine = mat[local[p], ro[n] % 8, pl.ds(64 * k, 64), :]
        leadh[t] = jnp.where(o_k[p] == k, mine, rcl[t])
        for q in range(16):
            dst1[q, t] = leadh[t, 4 * q : 4 * q + 4, :]
    rd1[me_plane] = dst1[me_plane]
    d1_args = (16, me_plane, lambda q: dst1.at[q], lambda q: rd1.at[q], plane, d1, e1)
    send_all(*d1_args)
    split_half.wait()
    for p in range(2):
        mine = mat[local[p], pl.ds(4 * k, 4)]
        half[pl.ds(4 * p, 4)] = jnp.where(o_k[p] == k, mine, rc1[p])

    rc2[me_xz] = half[z, pl.ds(64 * xh, 64), :]
    r2_args = (
        16, me_xz, lambda q: half.at[q % 8, pl.ds(64 * (q // 8), 64), :],
        lambda q: rc2.at[q], group, s2, r2,
    )
    send_all(*r2_args)

    recv_all(*d1_args)
    for t, (p, n) in enumerate(lead):
        slot = ro[n] // 8
        pd1[t] = rd1[(o_xh[p] * 2 + slot // 4) * 4 + slot % 4, t]
    rd2[z] = pd1[...]
    d2_args = (8, z, lambda q: pd1, lambda q: rd2.at[q], along, d2, e2)
    send_all(*d2_args)
    recv_all(*d2_args)
    for t, (p, n) in enumerate(lead):
        diag[k, me_plane, t] = rd2[o_z[p], t]
    d3_args = (16, me_plane, lambda q: diag.at[k, me_plane], lambda q: diag.at[k, q], plane, d3, e3)
    send_all(*d3_args)

    recv_all(*r2_args)
    src = jnp.where(z < 4, o_xh[0] * 8 + o_z[0], o_xh[1] * 8 + o_z[1])
    piece = rc2[src]
    pc2[...] = piece

    def rows_slot(q):
        zz = q % 8
        return rows.at[zz // 4, 4 * k + zz % 4, pl.ds(64 * (q // 8), 64), :]

    rows[z // 4, 4 * k + z % 4, pl.ds(64 * xh, 64), :] = piece
    r4_args = (16, me_xz, lambda q: pc2, rows_slot, group, s4, r4)
    send_all(*r4_args)

    recv_all(*d3_args)
    to_sibling(diag.at[k], diag.at[k], d4, e4).start()
    base = 2 * ((xh * 8 + z) * 2 + k)

    def find(n, carry):
        c = co[n]
        s = ro[n]
        return (
            carry[0] + jnp.where(c == base, s, 0),
            carry[1] + jnp.where(c == base + 1, s, 0),
        )

    slots = lax.fori_loop(0, NODES, find, (jnp.int32(0), jnp.int32(0)))
    joined_lead = to_sibling(diag.at[k], diag.at[1 - k], d4, e4)
    joined_lead.wait_send()
    joined_lead.wait_recv()

    rid = lax.broadcasted_iota(jnp.int32, (W, W), 0)
    cid = lax.broadcasted_iota(jnp.int32, (W, W), 1)
    eye = jnp.where(rid == cid, 1.0, 0.0).astype(F32)
    place_lead(diag, 0, wa)
    wb[...] = eye
    factor(wa, wb)
    low_out[0] = jnp.where(rid <= cid, wa[...], 0.0).T
    inv0 = wb[...]
    inv_out[0] = inv0
    place_lead(diag, 1, tile_a)
    f01 = nt(tile_a[...], inv0)
    f01_out[...] = f01
    place_lead(diag, 2, wa)
    wa[...] = wa[...] - nt(f01, f01)
    wb[...] = eye
    factor(wa, wb)
    low_out[1] = jnp.where(rid <= cid, wa[...], 0.0).T
    inv_out[1] = wb[...]

    recv_all(*r4_args)
    for p in range(2):
        mine = rows.at[p, pl.ds(4 * k, 4)]
        to_sibling(mine, mine, s5.at[p], r5.at[p]).start()
    for p in range(2):
        copy = to_sibling(
            rows.at[p, pl.ds(4 * k, 4)], rows.at[p, pl.ds(4 * (1 - k), 4)], s5.at[p], r5.at[p]
        )
        copy.wait_send()
        copy.wait_recv()

    for p in range(2):
        for l in range(2):
            tile = rows[p, slots[l] % 8]
            cst[4 * p + 2 * l] = tile[:64]
            cst[4 * p + 2 * l + 1] = tile[64:]
    rc3[me_row] = cst[me_row]
    c1_args = (8, me_row, lambda q: cst.at[q], lambda q: rc3.at[q], row_of, s6, r6)
    send_all(*c1_args)
    recv_all(*c1_args)
    from_row = jnp.where((me_row // 2) % 2 == 0, slots[0] // 8, slots[1] // 8)
    piece = rc3[from_row]
    pc3[...] = piece
    cols[me_row] = piece
    c2_args = (8, me_row, lambda q: pc3, lambda q: cols.at[q], row_of, s7, r7)
    send_all(*c2_args)
    rows_out[...] = rows[...]
    recv_all(*c2_args)
    cols_out[...] = cols[...]


def gather_tiles(mat, co, ro):
    vmem = pl.BlockSpec(memory_space=pltpu.VMEM)
    hbm = pl.BlockSpec(memory_space=pltpu.HBM)
    dma = pltpu.SemaphoreType.DMA
    vm = lambda *shape: pltpu.VMEM(shape, F32)
    pair = lambda n: [dma((n,)), dma((n,))]
    return pl.pallas_call(
        comm_kernel,
        out_shape=(
            jax.ShapeDtypeStruct((2, 8, W, W), F32),
            jax.ShapeDtypeStruct((8, 64, W), F32),
            jax.ShapeDtypeStruct((2, W, W), F32),
            jax.ShapeDtypeStruct((2, W, W), F32),
            jax.ShapeDtypeStruct((W, W), F32),
        ),
        in_specs=[hbm, hbm, hbm],
        out_specs=(vmem,) * 5,
        scratch_shapes=[
            vm(2, 8, W, W),
            pltpu.SMEM((NODES,), jnp.int32),
            pltpu.SMEM((NODES,), jnp.int32),
            vm(2, 4, W, W), vm(2, 4, W, W),
            vm(3, 64, W), vm(3, 64, W),
            vm(8, W, W), vm(3, 64, W),
            vm(16, 64, W), vm(64, W), vm(2, 8, W, W),
            vm(8, 64, W), vm(8, 64, W), vm(64, W), vm(8, 64, W),
            vm(16, 3, 4, W), vm(16, 3, 4, W), vm(3, 4, W), vm(8, 3, 4, W), vm(2, 16, 3, 4, W),
            vm(W, W), vm(W, W), vm(W, W),
            dma((3,)),
            *pair(2), *pair(16), *pair(16), *pair(2), *pair(8), *pair(8),
            *pair(16), *pair(8), *pair(16), dma, dma,
        ],
        compiler_params=pltpu.CompilerParams(
            collective_id=0, has_side_effects=True, vmem_limit_bytes=32 * 1024 * 1024
        ),
        name="gather_tiles",
    )(mat, co, ro)


def lanes(x):
    return jnp.broadcast_to(x, (x.shape[0], W))


def subs(x):
    return jnp.broadcast_to(x, (8, W))


def factor(wa_ref, wb_ref):
    rid = lax.broadcasted_iota(jnp.int32, (8, W), 0)
    for c in range(0, W, 8):
        wa = wa_ref[c : c + 8, :]
        wb = wb_ref[c : c + 8, :]
        cl = [lanes(wa[:, c + i : c + i + 1]) for i in range(8)]
        pa, pb, sc, lt = [], [], [], []
        for i in range(8):
            s = lax.rsqrt(subs(cl[i][i : i + 1]))
            li = cl[i] * s
            ra = subs(wa[i : i + 1]) * s
            rb = subs(wb[i : i + 1]) * s
            low = jnp.where(rid > i, li, 0.0)
            wa = jnp.where(rid == i, ra, wa - low * ra)
            wb = jnp.where(rid == i, rb, wb - low * rb)
            row = {}
            for j in range(i + 1, 8):
                row[j] = subs(li[j : j + 1])
                cl[j] = cl[j] - li * row[j]
            pa.append(ra)
            pb.append(rb)
            sc.append(s)
            lt.append(row)
        wa_ref[c : c + 8, :] = wa
        wb_ref[c : c + 8, :] = wb
        g = c + 8
        while g < W:
            size = min(16, W - g)
            tile = lambda v: jnp.concatenate([v] * (size // 8), axis=0) if size > 8 else v
            ga = wa_ref[g : g + size, :]
            gb = wb_ref[g : g + size, :]
            gc = [lanes(ga[:, c + i : c + i + 1]) for i in range(8)]
            for i in range(8):
                li = gc[i] * tile(sc[i])
                ga = ga - li * tile(pa[i])
                gb = gb - li * tile(pb[i])
                for j in range(i + 1, 8):
                    gc[j] = gc[j] - li * tile(lt[i][j])
            wa_ref[g : g + size, :] = ga
            wb_ref[g : g + size, :] = gb
            g += size


def nt(a, b):
    return lax.dot_general(a, b, (((1,), (1,)), ((), ())), precision=PRECISE, preferred_element_type=F32)


def nt16(a, b):
    return lax.dot_general(a, b, (((1,), (1,)), ((), ())), preferred_element_type=F32)


def parts(a):
    high = a.astype(jnp.bfloat16)
    return high, (a - high.astype(F32)).astype(jnp.bfloat16)


def nt3(a, b):
    ah, al = parts(a)
    bh, bl = parts(b)
    both = nt16(jnp.concatenate([ah, al], axis=1), jnp.concatenate([bh, bh], axis=1))
    return both + nt16(ah, bl)


def apply_kernel(mat, rows, cols, inv, low, f01, co, ro, pat, out, f0, f1, g0, g1, inv_row, inv_col):
    col = lax.axis_index("col")
    row = lax.axis_index("row")

    def invert(n, carry):
        inv_row[ro[n]] = n
        inv_col[co[n]] = n
        return carry

    lax.fori_loop(0, NODES, invert, 0)
    row_node = [inv_row[8 * row + s] for s in range(8)]
    col_node = [inv_col[2 * col + l] for l in range(2)]
    keep_row = [[pat[p, row_node[s]] == 1 for s in range(8)] for p in range(2)]
    keep_col = [[pat[p, col_node[l]] == 1 for l in range(2)] for p in range(2)]

    def mask(value, keeps):
        return jnp.concatenate(
            [jnp.where(keep, value[W * i : W * i + W], 0.0) for i, keep in enumerate(keeps)], axis=0
        )

    raw = lambda p: cols[4 * p : 4 * p + 4].reshape(2 * W, W)
    f0[...] = mask(nt3(rows[0].reshape(8 * W, W), inv[0]), keep_row[0])
    g0[...] = mask(nt3(raw(0), inv[0]), keep_col[0])
    f1[...] = mask(
        nt3(rows[1].reshape(8 * W, W) - nt3(f0[...], f01[...]), inv[1]), keep_row[1]
    )
    g1[...] = mask(nt3(raw(1) - nt3(g0[...], f01[...]), inv[1]), keep_col[1])
    g0h, g0l = parts(g0[...])
    g1h, g1l = parts(g1[...])
    gh = jnp.concatenate([g0h, g1h], axis=1)
    gl = jnp.concatenate([g0l, g1l], axis=1)
    for s in range(8):
        rows_s = slice(W * s, W * s + W)
        f0h, f0l = parts(f0[rows_s])
        f1h, f1l = parts(f1[rows_s])
        fh = jnp.concatenate([f0h, f1h], axis=1)
        fl = jnp.concatenate([f0l, f1l], axis=1)
        step = nt16(fh, gh) + nt16(fl, gh) + nt16(fh, gl)
        for l in range(2):
            old = mat[l, s]
            new = jnp.where(row_node[s] >= col_node[l], old - step[:, W * l : W * l + W], old)
            for p, f in enumerate((f0, f1)):
                here = col_node[l] == p
                new = jnp.where(here & keep_row[p][s], f[rows_s], new)
                new = jnp.where(here & (row_node[s] == p), low[p], new)
            out[l, s] = new


def apply_panels(mat, rows, cols, inv, low, f01, co, ro, pat):
    vmem = pl.BlockSpec(memory_space=pltpu.VMEM)
    smem = pl.BlockSpec(memory_space=pltpu.SMEM)
    return pl.pallas_call(
        apply_kernel,
        out_shape=jax.ShapeDtypeStruct((2, 8, W, W), F32),
        in_specs=[vmem] * 6 + [smem] * 3,
        out_specs=vmem,
        scratch_shapes=[
            pltpu.VMEM((8 * W, W), F32),
            pltpu.VMEM((8 * W, W), F32),
            pltpu.VMEM((2 * W, W), F32),
            pltpu.VMEM((2 * W, W), F32),
            pltpu.SMEM((NODES,), jnp.int32),
            pltpu.SMEM((NODES,), jnp.int32),
        ],
        compiler_params=pltpu.CompilerParams(vmem_limit_bytes=32 * 1024 * 1024),
        name="apply_panels",
    )(mat, rows, cols, inv, low, f01, co, ro, pat)


def body(matrix, col_owner, row_owner, pattern):
    found = gather_tiles(matrix, col_owner, row_owner)
    return apply_panels(matrix, *found, col_owner, row_owner, pattern)


def solution(mesh):
    return jax.shard_map(
        body,
        mesh=mesh,
        in_specs=(P("col", "row", None, None), P(), P(), P()),
        out_specs=P("col", "row", None, None),
        check_vma=False,
    )
```

```python
import functools

import jax
import jax.numpy as jnp
from jax import lax
from jax.experimental import pallas as pl
from jax.experimental.pallas import tpu as pltpu
from jax.sharding import PartitionSpec as P

MESH = pl.DeviceIdType.MESH
F32 = jnp.float32
PRECISE = lax.Precision.HIGHEST
W = 128
NODES = 64


def my_place():
    col = lax.axis_index("col")
    row = lax.axis_index("row")
    return col // 16, (col // 2) % 8, col % 2, row // 4, row % 4


def device(xh, z, k, xl, y):
    return {"col": (xh * 8 + z) * 2 + k, "row": xl * 4 + y}


def send_all(count, me, source, slot, target, send_sem, recv_sem):
    def step(q, carry):
        @pl.when(q != me)
        def _():
            pltpu.make_async_remote_copy(
                src_ref=source(q),
                dst_ref=slot(me),
                send_sem=send_sem.at[q],
                recv_sem=recv_sem.at[me],
                device_id=target(q),
                device_id_type=MESH,
            ).start()

        return carry

    lax.fori_loop(0, count, step, 0)


def recv_all(count, me, source, slot, target, send_sem, recv_sem):
    def step(q, carry):
        @pl.when(q != me)
        def _():
            copy = pltpu.make_async_remote_copy(
                src_ref=source(q),
                dst_ref=slot(q),
                send_sem=send_sem.at[q],
                recv_sem=recv_sem.at[q],
                device_id=target(q),
                device_id_type=MESH,
            )
            copy.wait_send()
            copy.wait_recv()

        return carry

    lax.fori_loop(0, count, step, 0)


def place_lead(diag, t, dst):
    for k in range(2):
        for q in range(16):
            dst[64 * k + 4 * q : 64 * k + 4 * q + 4, :] = diag[k, q, t]


FAR_FIRST = (4, 3, 5, 2, 6, 1, 7)


def comm_kernel(
    mat_hbm, co_hbm, ro_hbm, pat_hbm, base, fh, fl, inv, f01_out, cols, info,
    mat, co, ro, pat, st1, rc1, stl, rcl, half, leadh, rx, stz, rc2, pc2, za, xa, zb, xb, rows, cst, rc3, pc3, cbuf,
    dst1, rd1, pd1, rd2, diag, wa, wb, tile_a, low, f0,
    ld, s1, r1, sx, rxs, s2, r2, s4, r4, s4x, r4x, s5, r5, s6, r6, s7, r7,
    d1, e1, d2, e2, d3, e3, d4, e4,
):
    xh, z, k, xl, y = my_place()
    me_plane = (xh * 2 + xl) * 4 + y
    me_row = xl * 4 + y

    def plane(q):
        return device(q // 8, z, k, (q // 4) % 2, q % 4)

    def along(q):
        return device(xh, q, k, xl, y)

    def row_of(q):
        return device(xh, z, k, q // 4, q % 4)

    sib = device(xh, z, 1 - k, xl, y)
    partner = device(1 - xh, z, k, xl, y)

    def remote(src, dst, send, recv, target):
        return pltpu.make_async_remote_copy(
            src_ref=src, dst_ref=dst, send_sem=send, recv_sem=recv, device_id=target, device_id_type=MESH
        )

    barrier = pltpu.get_barrier_semaphore()

    def greet(count, me, target):
        def step(q, carry):
            @pl.when(q != me)
            def _():
                pl.semaphore_signal(barrier, inc=1, device_id=target(q), device_id_type=MESH)

            return carry

        lax.fori_loop(0, count, step, 0)

    greet(16, me_plane, plane)
    greet(8, z, along)
    pl.semaphore_signal(barrier, inc=1, device_id=sib, device_id_type=MESH)
    loads = [
        pltpu.make_async_copy(src, dst, ld.at[i])
        for i, (src, dst) in enumerate(((co_hbm, co), (ro_hbm, ro), (pat_hbm, pat), (mat_hbm, mat)))
    ]
    for copy in loads:
        copy.start()
    for copy in loads:
        copy.wait()

    owner = [co[p] // 2 for p in range(2)]
    local = [co[p] % 2 for p in range(2)]
    o_xh = [o // 16 for o in owner]
    o_z = [(o // 2) % 8 for o in owner]
    o_k = [o % 2 for o in owner]
    lead = ((0, 0), (0, 1), (1, 1))
    for p in range(2):
        st1[p] = mat[local[p], pl.ds(4 * (1 - k), 4)]
    for t, (p, n) in enumerate(lead):
        stl[t] = mat[local[p], ro[n] % 8, pl.ds(64 * (1 - k), 64), :]

    first_col = 2 * ((xh * 8 + z) * 2 + k)
    first_row = 8 * me_row

    def find(n, carry):
        c = co[n] - first_col
        s = ro[n]
        out = []
        for l in range(2):
            out.append(carry[l] + jnp.where(c == l, s, 0))
        for l in range(2):
            out.append(carry[2 + l] + jnp.where(c == l, n, 0))
        for i in range(8):
            out.append(carry[4 + i] + jnp.where(s - first_row == i, n, 0))
        return tuple(out)

    found = lax.fori_loop(0, NODES, find, (jnp.int32(0),) * 12)
    slots = [n % NODES for n in found[:2]]
    col_node = [n % NODES for n in found[2:4]]
    row_node = [n % NODES for n in found[4:]]
    keep_row = [[pat[p, n] == 1 for n in row_node] for p in range(2)]
    pl.semaphore_wait(barrier, 15 + 7 + 1)

    split_lead = remote(stl, rcl, s1.at[0], r1.at[0], sib)
    split_half = remote(st1, rc1, s1.at[1], r1.at[1], sib)
    split_lead.start()
    split_half.start()
    split_lead.wait()
    for t, (p, n) in enumerate(lead):
        mine = mat[local[p], ro[n] % 8, pl.ds(64 * k, 64), :]
        leadh[t] = jnp.where(o_k[p] == k, mine, rcl[t])
        for q in range(16):
            dst1[q, t] = leadh[t, 4 * q : 4 * q + 4, :]
    rd1[me_plane] = dst1[me_plane]
    d1_args = (16, me_plane, lambda q: dst1.at[q], lambda q: rd1.at[q], plane, d1, e1)
    send_all(*d1_args)
    split_half.wait()
    for p in range(2):
        mine = mat[local[p], pl.ds(4 * k, 4)]
        half[pl.ds(4 * p, 4)] = jnp.where(o_k[p] == k, mine, rc1[p])

    def cross(d):
        source = half.at[(z + d) % 8, pl.ds(64 * (1 - xh), 64), :]
        return remote(source, rx.at[d], sx.at[d], rxs.at[d], partner)

    def deal(d):
        return remote(stz.at[d], rc2.at[d], s2.at[d], r2.at[d], along((z + d) % 8))

    def scatter(d):
        zz = (z + d) % 8
        cross(d).wait_recv()
        own = jnp.where(zz < 4, o_xh[0], o_xh[1]) == xh
        value = jnp.where(own, half[zz, pl.ds(64 * xh, 64), :], rx[d])
        if d == 0:
            rc2[0] = value
        else:
            stz[d] = value
            deal(d).start()

    for d in FAR_FIRST + (0,):
        cross(d).start()
    for d in FAR_FIRST[:4]:
        scatter(d)
    recv_all(*d1_args)
    for t, (p, n) in enumerate(lead):
        slot = ro[n] // 8
        pd1[t] = rd1[(o_xh[p] * 2 + slot // 4) * 4 + slot % 4, t]
    rd2[z] = pd1[...]
    d2_args = (8, z, lambda q: pd1, lambda q: rd2.at[q], along, d2, e2)
    send_all(*d2_args)
    for d in FAR_FIRST[4:] + (0,):
        scatter(d)
    recv_all(*d2_args)
    for t, (p, n) in enumerate(lead):
        diag[k, me_plane, t] = rd2[o_z[p], t]
    d3_args = (16, me_plane, lambda q: diag.at[k, me_plane], lambda q: diag.at[k, q], plane, d3, e3)
    send_all(*d3_args)
    for d in FAR_FIRST:
        deal(d).wait()
    piece = rc2[(z + 8 - jnp.where(z < 4, o_z[0], o_z[1])) % 8]
    pc2[...] = piece

    def spread(d):
        return remote(pc2, za.at[d], s4.at[d], r4.at[d], along((z + d) % 8))

    def hand_over(d):
        return remote(za.at[d], xa.at[d], s4x.at[d], r4x.at[d], partner)

    za[0] = piece
    for d in FAR_FIRST:
        spread(d).start()
    hand_over(0).start()
    recv_all(*d3_args)
    remote(diag.at[k], diag.at[k], d4, e4, sib).start()

    for d in FAR_FIRST:
        spread(d).wait()
        hand_over(d).start()
    remote(za, zb, s5.at[0], r5.at[0], sib).start()
    joined_lead = remote(diag.at[k], diag.at[1 - k], d4, e4, sib)
    joined_lead.wait_send()
    joined_lead.wait_recv()

    rid = lax.broadcasted_iota(jnp.int32, (W, W), 0)
    cid = lax.broadcasted_iota(jnp.int32, (W, W), 1)
    eye = jnp.where(rid == cid, 1.0, 0.0).astype(F32)
    place_lead(diag, 0, wa)
    wb[...] = eye
    factor(wa, wb, 0, 6)

    for d in range(8):
        hand_over(d).wait()
        cross(d).wait_send()
    remote(xa, xb, s5.at[1], r5.at[1], sib).start()
    factor(wa, wb, 6, 16)
    low[0] = jnp.where(rid <= cid, wa[...], 0.0).T
    inv0 = wb[...]
    inv[0] = inv0
    remote(za, zb, s5.at[0], r5.at[0], sib).wait()
    remote(xa, xb, s5.at[1], r5.at[1], sib).wait()
    for d in range(8):
        t = (z + 8 - d) % 8
        for core, pieces in ((k, (za, xa)), (1 - k, (zb, xb))):
            rows[t // 4, 4 * core + t % 4, pl.ds(64 * xh, 64), :] = pieces[0][d]
            rows[t // 4, 4 * core + t % 4, pl.ds(64 * (1 - xh), 64), :] = pieces[1][d]

    for p in range(2):
        for l in range(2):
            tile = rows[p, slots[l] % 8]
            cst[4 * p + 2 * l] = tile[:64]
            cst[4 * p + 2 * l + 1] = tile[64:]
    rc3[me_row] = cst[me_row]
    c1_args = (8, me_row, lambda q: cst.at[q], lambda q: rc3.at[q], row_of, s6, r6)
    send_all(*c1_args)

    place_lead(diag, 1, tile_a)
    f01 = nt(tile_a[...], inv0)
    f01_out[...] = f01
    place_lead(diag, 2, wa)
    wa[...] = wa[...] - nt(f01, f01)
    wb[...] = eye
    factor(wa, wb, 0, 16)
    low[1] = jnp.where(rid <= cid, wa[...], 0.0).T
    inv[1] = wb[...]

    recv_all(*c1_args)
    piece = rc3[jnp.where((me_row // 2) % 2 == 0, slots[0] // 8, slots[1] // 8)]
    pc3[...] = piece
    cbuf[me_row] = piece
    c2_args = (8, me_row, lambda q: pc3, lambda q: cbuf.at[q], row_of, s7, r7)
    send_all(*c2_args)

    def mask(value, keeps):
        return jnp.concatenate(
            [jnp.where(keep, value[W * i : W * i + W], 0.0) for i, keep in enumerate(keeps)], axis=0
        )

    f0[...] = mask(nt3(rows[0].reshape(8 * W, W), inv[0]), keep_row[0])
    fh[:, :W], fl[:, :W] = parts(f0[...])
    f1 = mask(nt3(rows[1].reshape(8 * W, W) - nt3(f0[...], f01_out[...]), inv[1]), keep_row[1])
    fh[:, W:], fl[:, W:] = parts(f1)
    for l in range(2):
        first = col_node[l] == 0
        second = col_node[l] == 1
        for s in range(8):
            rows_s = slice(W * s, W * s + W)
            here = ((first & keep_row[0][s]), (second & keep_row[1][s]))
            edge = ((first & (row_node[s] == 0)), (second & (row_node[s] == 1)))
            tile = mat[l, s]
            tile = jnp.where(here[0], f0[rows_s], tile)
            tile = jnp.where(here[1], f1[rows_s], tile)
            tile = jnp.where(edge[0], low[0], tile)
            base[l, s] = jnp.where(edge[1], low[1], tile)
            fixed = here[0] | here[1] | edge[0] | edge[1]
            change = (row_node[s] >= col_node[l]) & jnp.logical_not(fixed)
            i = 8 * l + s
            info[i : i + 1, :] = jnp.where(change, jnp.ones((1, W), F32), 0.0)
    for p in range(2):
        for l in range(2):
            i = 16 + 2 * p + l
            info[i : i + 1, :] = jnp.where(pat[p, col_node[l]] == 1, jnp.ones((1, W), F32), 0.0)
    info[20:, :] = jnp.zeros((4, W), F32)
    recv_all(*c2_args)
    cols[...] = cbuf[...]


def gather_tiles(mat, co, ro, pat):
    vmem = pl.BlockSpec(memory_space=pltpu.VMEM)
    hbm = pl.BlockSpec(memory_space=pltpu.HBM)
    dma = pltpu.SemaphoreType.DMA
    vm = lambda *shape: pltpu.VMEM(shape, F32)
    pair = lambda n: [dma((n,)), dma((n,))]
    out = lambda *shape, dtype=F32: jax.ShapeDtypeStruct(shape, dtype)
    return pl.pallas_call(
        comm_kernel,
        out_shape=(
            out(2, 8, W, W),
            out(8 * W, 2 * W, dtype=jnp.bfloat16),
            out(8 * W, 2 * W, dtype=jnp.bfloat16),
            out(2, W, W),
            out(W, W),
            out(8, 64, W),
            out(24, W),
        ),
        in_specs=[hbm] * 4,
        out_specs=(vmem,) * 7,
        scratch_shapes=[
            vm(2, 8, W, W),
            pltpu.SMEM((NODES,), jnp.int32),
            pltpu.SMEM((NODES,), jnp.int32),
            pltpu.SMEM((2, NODES), jnp.int32),
            vm(2, 4, W, W), vm(2, 4, W, W),
            vm(3, 64, W), vm(3, 64, W),
            vm(8, W, W), vm(3, 64, W),
            vm(8, 64, W), vm(8, 64, W), vm(8, 64, W), vm(64, W),
            vm(8, 64, W), vm(8, 64, W), vm(8, 64, W), vm(8, 64, W), vm(2, 8, W, W),
            vm(8, 64, W), vm(8, 64, W), vm(64, W), vm(8, 64, W),
            vm(16, 3, 4, W), vm(16, 3, 4, W), vm(3, 4, W), vm(8, 3, 4, W), vm(2, 16, 3, 4, W),
            vm(W, W), vm(W, W), vm(W, W), vm(2, W, W), vm(8 * W, W),
            dma((4,)),
            *pair(2), *pair(8), *pair(8), *pair(8), *pair(8), *pair(2), *pair(8), *pair(8),
            *pair(16), *pair(8), *pair(16), dma, dma,
        ],
        compiler_params=pltpu.CompilerParams(
            collective_id=0, has_side_effects=True, vmem_limit_bytes=40 * 1024 * 1024
        ),
        name="gather_tiles",
    )(mat, co, ro, pat)


def lanes(x):
    return jnp.broadcast_to(x, (x.shape[0], W))


def subs(x):
    return jnp.broadcast_to(x, (8, W))


def factor(wa_ref, wb_ref, first, last):
    rid = lax.broadcasted_iota(jnp.int32, (8, W), 0)
    for c in range(8 * first, 8 * last, 8):
        wa = wa_ref[c : c + 8, :]
        wb = wb_ref[c : c + 8, :]
        cl = [lanes(wa[:, c + i : c + i + 1]) for i in range(8)]
        pa, pb, sc, lt = [], [], [], []
        for i in range(8):
            s = lax.rsqrt(subs(cl[i][i : i + 1]))
            li = cl[i] * s
            ra = subs(wa[i : i + 1]) * s
            rb = subs(wb[i : i + 1]) * s
            low = jnp.where(rid > i, li, 0.0)
            wa = jnp.where(rid == i, ra, wa - low * ra)
            wb = jnp.where(rid == i, rb, wb - low * rb)
            row = {}
            for j in range(i + 1, 8):
                row[j] = subs(li[j : j + 1])
                cl[j] = cl[j] - li * row[j]
            pa.append(ra)
            pb.append(rb)
            sc.append(s)
            lt.append(row)
        wa_ref[c : c + 8, :] = wa
        wb_ref[c : c + 8, :] = wb
        g = c + 8
        while g < W:
            size = min(16, W - g)
            tile = lambda v: jnp.concatenate([v] * (size // 8), axis=0) if size > 8 else v
            ga = wa_ref[g : g + size, :]
            gb = wb_ref[g : g + size, :]
            gc = [lanes(ga[:, c + i : c + i + 1]) for i in range(8)]
            for i in range(8):
                li = gc[i] * tile(sc[i])
                ga = ga - li * tile(pa[i])
                gb = gb - li * tile(pb[i])
                for j in range(i + 1, 8):
                    gc[j] = gc[j] - li * tile(lt[i][j])
            wa_ref[g : g + size, :] = ga
            wb_ref[g : g + size, :] = gb
            g += size


def nt(a, b):
    return lax.dot_general(a, b, (((1,), (1,)), ((), ())), precision=PRECISE, preferred_element_type=F32)


def nt16(a, b):
    return lax.dot_general(a, b, (((1,), (1,)), ((), ())), preferred_element_type=F32)


def parts(a):
    high = a.astype(jnp.bfloat16)
    return high, (a - high.astype(F32)).astype(jnp.bfloat16)


def nt3(a, b):
    ah, al = parts(a)
    bh, bl = parts(b)
    both = nt16(jnp.concatenate([ah, al], axis=1), jnp.concatenate([bh, bh], axis=1))
    return both + nt16(ah, bl)


def apply_kernel(base, fh, fl, inv, f01, cols, info, out, buf, sem):
    def flag(i):
        return info[i : i + 1, :] > 0.5

    def mask(value, p):
        return jnp.concatenate(
            [jnp.where(flag(16 + 2 * p + l), value[W * l : W * l + W], 0.0) for l in range(2)], axis=0
        )

    raw = lambda p: cols[4 * p : 4 * p + 4].reshape(2 * W, W)
    g0 = mask(nt3(raw(0), inv[0]), 0)
    g1 = mask(nt3(raw(1) - nt3(g0, f01[...]), inv[1]), 1)
    g0h, g0l = parts(g0)
    g1h, g1l = parts(g1)
    gh = jnp.concatenate([g0h, g1h], axis=1)
    gl = jnp.concatenate([g0l, g1l], axis=1)
    copies = []
    for s in range(0, 8, 2):
        both = slice(W * s, W * s + 2 * W)
        step = nt16(fh[both], gh) + nt16(fl[both], gh) + nt16(fh[both], gl)
        for l in range(2):
            for i in range(2):
                old = base[l, s + i]
                new = old - step[W * i : W * i + W, W * l : W * l + W]
                buf[l, s + i] = jnp.where(flag(8 * l + s + i), new, old)
            copy = pltpu.make_async_copy(buf.at[l, pl.ds(s, 2)], out.at[l, pl.ds(s, 2)], sem.at[l + s])
            copy.start()
            copies.append(copy)
    for copy in copies:
        copy.wait()


def apply_panels(base, fh, fl, inv, f01, cols, info):
    vmem = pl.BlockSpec(memory_space=pltpu.VMEM)
    return pl.pallas_call(
        apply_kernel,
        out_shape=jax.ShapeDtypeStruct((2, 8, W, W), F32),
        in_specs=[vmem] * 7,
        out_specs=pl.BlockSpec(memory_space=pltpu.HBM),
        scratch_shapes=[pltpu.VMEM((2, 8, W, W), F32), pltpu.SemaphoreType.DMA((8,))],
        compiler_params=pltpu.CompilerParams(vmem_limit_bytes=16 * 1024 * 1024),
        name="apply_panels",
    )(base, fh, fl, inv, f01, cols, info)


def body(matrix, col_owner, row_owner, pattern):
    held = [pltpu.with_memory_space_constraint(x, pltpu.HBM) for x in (matrix, col_owner, row_owner, pattern)]
    return apply_panels(*gather_tiles(*held))


def solution(mesh):
    return jax.shard_map(
        body,
        mesh=mesh,
        in_specs=(P("col", "row", None, None), P(), P(), P()),
        out_specs=P("col", "row", None, None),
        check_vma=False,
    )
```

```python
import functools

import jax
import jax.numpy as jnp
from jax import lax
from jax.experimental import pallas as pl
from jax.experimental.pallas import tpu as pltpu
from jax.sharding import PartitionSpec as P

MESH = pl.DeviceIdType.MESH
F32 = jnp.float32
PRECISE = lax.Precision.HIGHEST
W = 128
NODES = 64


def my_place():
    col = lax.axis_index("col")
    row = lax.axis_index("row")
    return col // 16, (col // 2) % 8, col % 2, row // 4, row % 4


def device(xh, z, k, xl, y):
    return {"col": (xh * 8 + z) * 2 + k, "row": xl * 4 + y}


def send_all(count, me, source, slot, target, send_sem, recv_sem):
    def step(q, carry):
        @pl.when(q != me)
        def _():
            pltpu.make_async_remote_copy(
                src_ref=source(q),
                dst_ref=slot(me),
                send_sem=send_sem.at[q],
                recv_sem=recv_sem.at[me],
                device_id=target(q),
                device_id_type=MESH,
            ).start()

        return carry

    lax.fori_loop(0, count, step, 0)


def wait_all(count, me, source, slot, target, send_sem, recv_sem, sent=False):
    def step(q, carry):
        @pl.when(q != me)
        def _():
            copy = pltpu.make_async_remote_copy(
                src_ref=source(q),
                dst_ref=slot(q),
                send_sem=send_sem.at[q],
                recv_sem=recv_sem.at[q],
                device_id=target(q),
                device_id_type=MESH,
            )
            if sent:
                copy.wait_send()
            else:
                copy.wait_recv()

        return carry

    lax.fori_loop(0, count, step, 0)


def recv_all(*args):
    wait_all(*args)


def sent_all(*args):
    wait_all(*args, sent=True)


def place_lead(diag, t, dst):
    for k in range(2):
        for q in range(16):
            dst[64 * k + 4 * q : 64 * k + 4 * q + 4, :] = diag[k, q, t]


FAR_FIRST = (4, 3, 5, 2, 6, 1, 7)


def comm_kernel(
    mat_hbm, co_hbm, ro_hbm, pat_hbm, base, fh, fl, inv, f01_out, cols, info,
    mat, co, ro, pat, st1, rc1, stl, rcl, half, leadh, rows,
    rx0, rx1, stz0, stz1, rc20, rc21, pc20, pc21, za0, za1, xa0, xa1, zb0, zb1, xb0, xb1,
    cst0, cst1, rc30, rc31, pc30, pc31, cbuf0, cbuf1,
    dst1, rd1, pd1, rd2, diag, wa, wb, tile_a, low, f0,
    ld, s1, r1, sx, rxs, s2, r2, s4, r4, s4x, r4x, s5, r5, s6, r6, s7, r7,
    d1, e1, d2, e2, d3, e3, d4, e4,
):
    rx, stz, rc2, pc2 = (rx0, rx1), (stz0, stz1), (rc20, rc21), (pc20, pc21)
    za, xa, zb, xb = (za0, za1), (xa0, xa1), (zb0, zb1), (xb0, xb1)
    cst, rc3, pc3, cbuf = (cst0, cst1), (rc30, rc31), (pc30, pc31), (cbuf0, cbuf1)
    waves = (0, 1)
    xh, z, k, xl, y = my_place()
    me_plane = (xh * 2 + xl) * 4 + y
    me_row = xl * 4 + y

    def plane(q):
        return device(q // 8, z, k, (q // 4) % 2, q % 4)

    def along(q):
        return device(xh, q, k, xl, y)

    def row_of(q):
        return device(xh, z, k, q // 4, q % 4)

    sib = device(xh, z, 1 - k, xl, y)
    partner = device(1 - xh, z, k, xl, y)

    def remote(src, dst, send, recv, target):
        return pltpu.make_async_remote_copy(
            src_ref=src, dst_ref=dst, send_sem=send, recv_sem=recv, device_id=target, device_id_type=MESH
        )

    loads = [
        pltpu.make_async_copy(src, dst, ld.at[i])
        for i, (src, dst) in enumerate(((co_hbm, co), (ro_hbm, ro), (pat_hbm, pat), (mat_hbm, mat)))
    ]
    for copy in loads:
        copy.start()

    barrier = pltpu.get_barrier_semaphore()

    def greet(count, me, target):
        def step(q, carry):
            @pl.when(q != me)
            def _():
                pl.semaphore_signal(barrier, inc=1, device_id=target(q), device_id_type=MESH)

            return carry

        lax.fori_loop(0, count, step, 0)

    greet(16, me_plane, plane)
    greet(8, z, along)
    pl.semaphore_signal(barrier, inc=1, device_id=sib, device_id_type=MESH)
    for copy in loads:
        copy.wait()

    owner = [co[p] // 2 for p in range(2)]
    local = [co[p] % 2 for p in range(2)]
    o_xh = [o // 16 for o in owner]
    o_z = [(o // 2) % 8 for o in owner]
    o_k = [o % 2 for o in owner]
    lead = ((0, 0), (0, 1), (1, 1))
    for p in range(2):
        st1[p] = mat[local[p], pl.ds(4 * (1 - k), 4)]
    for t, (p, n) in enumerate(lead):
        stl[t] = mat[local[p], ro[n] % 8, pl.ds(64 * (1 - k), 64), :]

    pl.semaphore_wait(barrier, 15 + 7 + 1)

    split_lead = remote(stl, rcl, s1.at[0], r1.at[0], sib)
    split_half = remote(st1, rc1, s1.at[1], r1.at[1], sib)
    split_lead.start()
    split_half.start()
    split_lead.wait_recv()
    for t, (p, n) in enumerate(lead):
        mine = mat[local[p], ro[n] % 8, pl.ds(64 * k, 64), :]
        leadh[t] = jnp.where(o_k[p] == k, mine, rcl[t])
        for q in range(16):
            dst1[q, t] = leadh[t, 4 * q : 4 * q + 4, :]
    rd1[me_plane] = dst1[me_plane]
    d1_args = (16, me_plane, lambda q: dst1.at[q], lambda q: rd1.at[q], plane, d1, e1)
    send_all(*d1_args)
    split_half.wait_recv()
    for p in range(2):
        mine = mat[local[p], pl.ds(4 * k, 4)]
        half[pl.ds(4 * p, 4)] = jnp.where(o_k[p] == k, mine, rc1[p])

    def cross(d, w):
        source = half.at[(z + d) % 8, pl.ds(64 * (1 - xh) + 32 * w, 32), :]
        return remote(source, rx[w].at[d], sx.at[w, d], rxs.at[w, d], partner)

    def deal(d, w):
        return remote(stz[w].at[d], rc2[w].at[d], s2.at[w, d], r2.at[w, d], along((z + d) % 8))

    def scatter(d, w):
        zz = (z + d) % 8
        cross(d, w).wait_recv()
        own = jnp.where(zz < 4, o_xh[0], o_xh[1]) == xh
        value = jnp.where(own, half[zz, pl.ds(64 * xh + 32 * w, 32), :], rx[w][d])
        if d == 0:
            rc2[w][0] = value
        else:
            stz[w][d] = value
            deal(d, w).start()

    for w in waves:
        for d in FAR_FIRST + (0,):
            cross(d, w).start()

    first_col = 2 * ((xh * 8 + z) * 2 + k)
    first_row = 8 * me_row

    def find(n, carry):
        c = co[n] - first_col
        s = ro[n]
        out = []
        for l in range(2):
            out.append(carry[l] + jnp.where(c == l, s, 0))
        for l in range(2):
            out.append(carry[2 + l] + jnp.where(c == l, n, 0))
        for i in range(8):
            out.append(carry[4 + i] + jnp.where(s - first_row == i, n, 0))
        return tuple(out)

    found = lax.fori_loop(0, NODES, find, (jnp.int32(0),) * 12)
    slots = [n % NODES for n in found[:2]]
    col_node = [n % NODES for n in found[2:4]]
    row_node = [n % NODES for n in found[4:]]
    keep_row = [[pat[p, n] == 1 for n in row_node] for p in range(2)]

    for d in FAR_FIRST + (0,):
        scatter(d, 0)
    recv_all(*d1_args)
    for t, (p, n) in enumerate(lead):
        slot = ro[n] // 8
        pd1[t] = rd1[(o_xh[p] * 2 + slot // 4) * 4 + slot % 4, t]
    rd2[z] = pd1[...]
    d2_args = (8, z, lambda q: pd1, lambda q: rd2.at[q], along, d2, e2)
    send_all(*d2_args)
    for d in FAR_FIRST + (0,):
        scatter(d, 1)

    def spread(d, w):
        return remote(pc2[w], za[w].at[d], s4.at[w, d], r4.at[w, d], along((z + d) % 8))

    def hand_over(d, w):
        return remote(za[w].at[d], xa[w].at[d], s4x.at[w, d], r4x.at[w, d], partner)

    def start_gather(w):
        for d in FAR_FIRST:
            deal(d, w).wait_recv()
        piece = rc2[w][(z + 8 - jnp.where(z < 4, o_z[0], o_z[1])) % 8]
        pc2[w][...] = piece
        za[w][0] = piece
        for d in FAR_FIRST:
            spread(d, w).start()
        hand_over(0, w).start()

    start_gather(0)
    recv_all(*d2_args)
    for t, (p, n) in enumerate(lead):
        diag[k, me_plane, t] = rd2[o_z[p], t]
    d3_args = (16, me_plane, lambda q: diag.at[k, me_plane], lambda q: diag.at[k, q], plane, d3, e3)
    send_all(*d3_args)
    start_gather(1)
    recv_all(*d3_args)
    remote(diag.at[k], diag.at[k], d4, e4, sib).start()

    def join(src, dst, i, w):
        return remote(src[w], dst[w], s5.at[i, w], r5.at[i, w], sib)

    for w in waves:
        for d in FAR_FIRST:
            spread(d, w).wait_recv()
            hand_over(d, w).start()
        join(za, zb, 0, w).start()
    joined_lead = remote(diag.at[k], diag.at[1 - k], d4, e4, sib)
    joined_lead.wait_recv()

    rid = lax.broadcasted_iota(jnp.int32, (W, W), 0)
    cid = lax.broadcasted_iota(jnp.int32, (W, W), 1)
    eye = jnp.where(rid == cid, 1.0, 0.0).astype(F32)
    place_lead(diag, 0, wa)
    wb[...] = eye
    factor(wa, wb, 0, 4)

    def crossed(w):
        for d in range(8):
            hand_over(d, w).wait_recv()
        join(xa, xb, 1, w).start()

    def c1_args(w):
        return 8, me_row, lambda q: cst[w].at[q], lambda q: rc3[w].at[q], row_of, s6.at[w], r6.at[w]

    def c2_args(w):
        return 8, me_row, lambda q: pc3[w], lambda q: cbuf[w].at[q], row_of, s7.at[w], r7.at[w]

    def start_columns(w):
        join(za, zb, 0, w).wait_recv()
        join(xa, xb, 1, w).wait_recv()
        for p in range(2):
            for l in range(2):
                i = slots[l] % 8
                d = (z + 8 - 4 * p - i % 4) % 8
                mine = i // 4 == k
                cst[w][4 * p + 2 * l + xh] = jnp.where(mine, za[w][d], zb[w][d])
                cst[w][4 * p + 2 * l + 1 - xh] = jnp.where(mine, xa[w][d], xb[w][d])
        rc3[w][me_row] = cst[w][me_row]
        send_all(*c1_args(w))

    def pass_columns(w):
        recv_all(*c1_args(w))
        piece = rc3[w][jnp.where((me_row // 2) % 2 == 0, slots[0] // 8, slots[1] // 8)]
        pc3[w][...] = piece
        cbuf[w][me_row] = piece
        send_all(*c2_args(w))

    crossed(0)
    factor(wa, wb, 4, 8)
    crossed(1)
    start_columns(0)
    start_columns(1)
    factor(wa, wb, 8, 16)
    low[0] = jnp.where(rid <= cid, wa[...], 0.0).T
    inv0 = wb[...]
    inv[0] = inv0
    place_lead(diag, 1, tile_a)
    f01 = nt(tile_a[...], inv0)
    f01_out[...] = f01
    place_lead(diag, 2, wa)
    wa[...] = wa[...] - nt(f01, f01)
    wb[...] = eye
    factor(wa, wb, 0, 16)
    low[1] = jnp.where(rid <= cid, wa[...], 0.0).T
    inv[1] = wb[...]

    pass_columns(0)
    pass_columns(1)
    for d in range(8):
        t = (z + 8 - d) % 8
        for w in waves:
            for core, pieces in ((k, (za, xa)), (1 - k, (zb, xb))):
                rows[t // 4, 4 * core + t % 4, pl.ds(64 * xh + 32 * w, 32), :] = pieces[0][w][d]
                rows[t // 4, 4 * core + t % 4, pl.ds(64 * (1 - xh) + 32 * w, 32), :] = pieces[1][w][d]

    def mask(value, keeps):
        return jnp.concatenate(
            [jnp.where(keep, value[W * i : W * i + W], 0.0) for i, keep in enumerate(keeps)], axis=0
        )

    f0[...] = mask(nt3(rows[0].reshape(8 * W, W), inv[0]), keep_row[0])
    fh[:, :W], fl[:, :W] = parts(f0[...])
    f1 = mask(nt3(rows[1].reshape(8 * W, W) - nt3(f0[...], f01_out[...]), inv[1]), keep_row[1])
    fh[:, W:], fl[:, W:] = parts(f1)
    for l in range(2):
        first = col_node[l] == 0
        second = col_node[l] == 1
        for s in range(8):
            rows_s = slice(W * s, W * s + W)
            here = ((first & keep_row[0][s]), (second & keep_row[1][s]))
            edge = ((first & (row_node[s] == 0)), (second & (row_node[s] == 1)))
            tile = mat[l, s]
            tile = jnp.where(here[0], f0[rows_s], tile)
            tile = jnp.where(here[1], f1[rows_s], tile)
            tile = jnp.where(edge[0], low[0], tile)
            base[l, s] = jnp.where(edge[1], low[1], tile)
            fixed = here[0] | here[1] | edge[0] | edge[1]
            change = (row_node[s] >= col_node[l]) & jnp.logical_not(fixed)
            i = 8 * l + s
            info[i : i + 1, :] = jnp.where(change, jnp.ones((1, W), F32), 0.0)
    for p in range(2):
        for l in range(2):
            i = 16 + 2 * p + l
            info[i : i + 1, :] = jnp.where(pat[p, col_node[l]] == 1, jnp.ones((1, W), F32), 0.0)
    info[20:, :] = jnp.zeros((4, W), F32)
    for arguments in (d1_args, d2_args, d3_args, c1_args(0), c1_args(1), c2_args(0), c2_args(1)):
        sent_all(*arguments)
    for w in waves:
        for d in range(8):
            cross(d, w).wait_send()
            hand_over(d, w).wait_send()
            if d:
                deal(d, w).wait_send()
                spread(d, w).wait_send()
        join(za, zb, 0, w).wait_send()
        join(xa, xb, 1, w).wait_send()
    for copy in (split_lead, split_half, joined_lead):
        copy.wait_send()
    for w in waves:
        recv_all(*c2_args(w))
        for q in range(8):
            cols[q, 32 * w : 32 * w + 32, :] = cbuf[w][q]


def gather_tiles(mat, co, ro, pat):
    vmem = pl.BlockSpec(memory_space=pltpu.VMEM)
    hbm = pl.BlockSpec(memory_space=pltpu.HBM)
    dma = pltpu.SemaphoreType.DMA
    vm = lambda *shape: pltpu.VMEM(shape, F32)
    pair = lambda n: [dma((n,)), dma((n,))]
    pairs = lambda n: [dma((2, n)), dma((2, n))]
    out = lambda *shape, dtype=F32: jax.ShapeDtypeStruct(shape, dtype)
    return pl.pallas_call(
        comm_kernel,
        out_shape=(
            out(2, 8, W, W),
            out(8 * W, 2 * W, dtype=jnp.bfloat16),
            out(8 * W, 2 * W, dtype=jnp.bfloat16),
            out(2, W, W),
            out(W, W),
            out(8, 64, W),
            out(24, W),
        ),
        in_specs=[hbm] * 4,
        out_specs=(vmem,) * 7,
        scratch_shapes=[
            vm(2, 8, W, W),
            pltpu.SMEM((NODES,), jnp.int32),
            pltpu.SMEM((NODES,), jnp.int32),
            pltpu.SMEM((2, NODES), jnp.int32),
            vm(2, 4, W, W), vm(2, 4, W, W),
            vm(3, 64, W), vm(3, 64, W),
            vm(8, W, W), vm(3, 64, W), vm(2, 8, W, W),
            *[vm(8, 32, W)] * 6, *[vm(32, W)] * 2, *[vm(8, 32, W)] * 8,
            *[vm(8, 32, W)] * 4, *[vm(32, W)] * 2, *[vm(8, 32, W)] * 2,
            vm(16, 3, 4, W), vm(16, 3, 4, W), vm(3, 4, W), vm(8, 3, 4, W), vm(2, 16, 3, 4, W),
            vm(W, W), vm(W, W), vm(W, W), vm(2, W, W), vm(8 * W, W),
            dma((4,)),
            *pair(2), *pairs(8), *pairs(8), *pairs(8), *pairs(8), *pairs(2), *pairs(8), *pairs(8),
            *pair(16), *pair(8), *pair(16), dma, dma,
        ],
        compiler_params=pltpu.CompilerParams(
            collective_id=0, has_side_effects=True, vmem_limit_bytes=40 * 1024 * 1024
        ),
        name="gather_tiles",
    )(mat, co, ro, pat)


def lanes(x):
    return jnp.broadcast_to(x, (x.shape[0], W))


def subs(x):
    return jnp.broadcast_to(x, (8, W))


def factor(wa_ref, wb_ref, first, last):
    rid = lax.broadcasted_iota(jnp.int32, (8, W), 0)
    for c in range(8 * first, 8 * last, 8):
        wa = wa_ref[c : c + 8, :]
        wb = wb_ref[c : c + 8, :]
        cl = [lanes(wa[:, c + i : c + i + 1]) for i in range(8)]
        pa, pb, sc, lt = [], [], [], []
        for i in range(8):
            s = lax.rsqrt(subs(cl[i][i : i + 1]))
            li = cl[i] * s
            ra = subs(wa[i : i + 1]) * s
            rb = subs(wb[i : i + 1]) * s
            low = jnp.where(rid > i, li, 0.0)
            wa = jnp.where(rid == i, ra, wa - low * ra)
            wb = jnp.where(rid == i, rb, wb - low * rb)
            row = {}
            for j in range(i + 1, 8):
                row[j] = subs(li[j : j + 1])
                cl[j] = cl[j] - li * row[j]
            pa.append(ra)
            pb.append(rb)
            sc.append(s)
            lt.append(row)
        wa_ref[c : c + 8, :] = wa
        wb_ref[c : c + 8, :] = wb
        g = c + 8
        while g < W:
            size = min(16, W - g)
            tile = lambda v: jnp.concatenate([v] * (size // 8), axis=0) if size > 8 else v
            ga = wa_ref[g : g + size, :]
            gb = wb_ref[g : g + size, :]
            gc = [lanes(ga[:, c + i : c + i + 1]) for i in range(8)]
            for i in range(8):
                li = gc[i] * tile(sc[i])
                ga = ga - li * tile(pa[i])
                gb = gb - li * tile(pb[i])
                for j in range(i + 1, 8):
                    gc[j] = gc[j] - li * tile(lt[i][j])
            wa_ref[g : g + size, :] = ga
            wb_ref[g : g + size, :] = gb
            g += size


def nt(a, b):
    return lax.dot_general(a, b, (((1,), (1,)), ((), ())), precision=PRECISE, preferred_element_type=F32)


def nt16(a, b):
    return lax.dot_general(a, b, (((1,), (1,)), ((), ())), preferred_element_type=F32)


def parts(a):
    high = a.astype(jnp.bfloat16)
    return high, (a - high.astype(F32)).astype(jnp.bfloat16)


def nt3(a, b):
    ah, al = parts(a)
    bh, bl = parts(b)
    both = nt16(jnp.concatenate([ah, al], axis=1), jnp.concatenate([bh, bh], axis=1))
    return both + nt16(ah, bl)


def apply_kernel(base, fh, fl, inv, f01, cols, info, out, buf, sem):
    def flag(i):
        return info[i : i + 1, :] > 0.5

    def mask(value, p):
        return jnp.concatenate(
            [jnp.where(flag(16 + 2 * p + l), value[W * l : W * l + W], 0.0) for l in range(2)], axis=0
        )

    raw = lambda p: cols[4 * p : 4 * p + 4].reshape(2 * W, W)
    g0 = mask(nt3(raw(0), inv[0]), 0)
    g1 = mask(nt3(raw(1) - nt3(g0, f01[...]), inv[1]), 1)
    g0h, g0l = parts(g0)
    g1h, g1l = parts(g1)
    gh = jnp.concatenate([g0h, g1h], axis=1)
    gl = jnp.concatenate([g0l, g1l], axis=1)
    copies = []
    for s in range(0, 8, 2):
        both = slice(W * s, W * s + 2 * W)
        step = nt16(fh[both], gh) + nt16(fl[both], gh) + nt16(fh[both], gl)
        for l in range(2):
            for i in range(2):
                old = base[l, s + i]
                new = old - step[W * i : W * i + W, W * l : W * l + W]
                buf[l, s + i] = jnp.where(flag(8 * l + s + i), new, old)
            copy = pltpu.make_async_copy(buf.at[l, pl.ds(s, 2)], out.at[l, pl.ds(s, 2)], sem.at[l + s])
            copy.start()
            copies.append(copy)
    for copy in copies:
        copy.wait()


def apply_panels(base, fh, fl, inv, f01, cols, info):
    vmem = pl.BlockSpec(memory_space=pltpu.VMEM)
    return pl.pallas_call(
        apply_kernel,
        out_shape=jax.ShapeDtypeStruct((2, 8, W, W), F32),
        in_specs=[vmem] * 7,
        out_specs=pl.BlockSpec(memory_space=pltpu.HBM),
        scratch_shapes=[pltpu.VMEM((2, 8, W, W), F32), pltpu.SemaphoreType.DMA((8,))],
        compiler_params=pltpu.CompilerParams(vmem_limit_bytes=16 * 1024 * 1024),
        name="apply_panels",
    )(base, fh, fl, inv, f01, cols, info)


def body(matrix, col_owner, row_owner, pattern):
    held = [pltpu.with_memory_space_constraint(x, pltpu.HBM) for x in (matrix, col_owner, row_owner, pattern)]
    return apply_panels(*gather_tiles(*held))


def solution(mesh):
    return jax.shard_map(
        body,
        mesh=mesh,
        in_specs=(P("col", "row", None, None), P(), P(), P()),
        out_specs=P("col", "row", None, None),
        check_vma=False,
    )
```

```python
import functools

import jax
import jax.numpy as jnp
from jax import lax
from jax.experimental import pallas as pl
from jax.experimental.pallas import tpu as pltpu
from jax.sharding import PartitionSpec as P

MESH = pl.DeviceIdType.MESH
F32 = jnp.float32
PRECISE = lax.Precision.HIGHEST
W = 128
NODES = 64


def my_place():
    col = lax.axis_index("col")
    row = lax.axis_index("row")
    return col // 16, (col // 2) % 8, col % 2, row // 4, row % 4


def device(xh, z, k, xl, y):
    return {"col": (xh * 8 + z) * 2 + k, "row": xl * 4 + y}


def send_all(count, me, source, slot, target, send_sem, recv_sem):
    def step(q, carry):
        @pl.when(q != me)
        def _():
            pltpu.make_async_remote_copy(
                src_ref=source(q),
                dst_ref=slot(me),
                send_sem=send_sem.at[q],
                recv_sem=recv_sem.at[me],
                device_id=target(q),
                device_id_type=MESH,
            ).start()

        return carry

    lax.fori_loop(0, count, step, 0)


def wait_all(count, me, source, slot, target, send_sem, recv_sem, sent=False):
    def step(q, carry):
        @pl.when(q != me)
        def _():
            copy = pltpu.make_async_remote_copy(
                src_ref=source(q),
                dst_ref=slot(q),
                send_sem=send_sem.at[q],
                recv_sem=recv_sem.at[q],
                device_id=target(q),
                device_id_type=MESH,
            )
            if sent:
                copy.wait_send()
            else:
                copy.wait_recv()

        return carry

    lax.fori_loop(0, count, step, 0)


def recv_all(*args):
    wait_all(*args)


def sent_all(*args):
    wait_all(*args, sent=True)


def place_lead(diag, t, dst):
    for k in range(2):
        for q in range(16):
            dst[64 * k + 4 * q : 64 * k + 4 * q + 4, :] = diag[k, q, t]


FAR_FIRST = (4, 3, 5, 2, 6, 1, 7)


def comm_kernel(
    mat_hbm, co_hbm, ro_hbm, pat_hbm, base, fh, fl, inv, f01_out, cols, info,
    mat, co, ro, pat, st1, rc1, stl, rcl, half, leadh, rows,
    rx0, rx1, stz0, stz1, rc20, rc21, pc20, pc21, za0, za1, xa0, xa1, zb0, zb1, xb0, xb1,
    cst0, cst1, rc30, rc31, pc30, pc31, cbuf0, cbuf1,
    dst1, rd1, pd1, rd2, diag, wa, wb, tile_a, low, f0,
    ld, s1, r1, sx, rxs, s2, r2, s4, r4, s4x, r4x, s5, r5, s6, r6, s7, r7,
    d1, e1, d2, e2, d3, e3, d4, e4,
):
    rx, stz, rc2, pc2 = (rx0, rx1), (stz0, stz1), (rc20, rc21), (pc20, pc21)
    za, xa, zb, xb = (za0, za1), (xa0, xa1), (zb0, zb1), (xb0, xb1)
    cst, rc3, pc3, cbuf = (cst0, cst1), (rc30, rc31), (pc30, pc31), (cbuf0, cbuf1)
    waves = (0, 1)
    xh, z, k, xl, y = my_place()
    me_plane = (xh * 2 + xl) * 4 + y
    me_row = xl * 4 + y

    def plane(q):
        return device(q // 8, z, k, (q // 4) % 2, q % 4)

    def along(q):
        return device(xh, q, k, xl, y)

    def row_of(q):
        return device(xh, z, k, q // 4, q % 4)

    sib = device(xh, z, 1 - k, xl, y)
    partner = device(1 - xh, z, k, xl, y)

    def remote(src, dst, send, recv, target):
        return pltpu.make_async_remote_copy(
            src_ref=src, dst_ref=dst, send_sem=send, recv_sem=recv, device_id=target, device_id_type=MESH
        )

    loads = [
        pltpu.make_async_copy(src, dst, ld.at[i])
        for i, (src, dst) in enumerate(((co_hbm, co), (ro_hbm, ro), (pat_hbm, pat), (mat_hbm, mat)))
    ]
    for copy in loads:
        copy.start()

    barrier = pltpu.get_barrier_semaphore()

    def greet(count, me, target):
        def step(q, carry):
            @pl.when(q != me)
            def _():
                pl.semaphore_signal(barrier, inc=1, device_id=target(q), device_id_type=MESH)

            return carry

        lax.fori_loop(0, count, step, 0)

    greet(16, me_plane, plane)
    greet(8, z, along)
    pl.semaphore_signal(barrier, inc=1, device_id=sib, device_id_type=MESH)
    for copy in loads:
        copy.wait()

    owner = [co[p] // 2 for p in range(2)]
    local = [co[p] % 2 for p in range(2)]
    o_xh = [o // 16 for o in owner]
    o_z = [(o // 2) % 8 for o in owner]
    o_k = [o % 2 for o in owner]
    lead = ((0, 0), (0, 1), (1, 1))
    for p in range(2):
        st1[p] = mat[local[p], pl.ds(4 * (1 - k), 4)]
    for t, (p, n) in enumerate(lead):
        stl[t] = mat[local[p], ro[n] % 8, pl.ds(64 * (1 - k), 64), :]

    pl.semaphore_wait(barrier, 15 + 7 + 1)

    split_lead = remote(stl, rcl, s1.at[0], r1.at[0], sib)
    split_half = remote(st1, rc1, s1.at[1], r1.at[1], sib)
    split_lead.start()
    split_half.start()
    split_lead.wait_recv()
    for t, (p, n) in enumerate(lead):
        mine = mat[local[p], ro[n] % 8, pl.ds(64 * k, 64), :]
        leadh[t] = jnp.where(o_k[p] == k, mine, rcl[t])
        for q in range(16):
            dst1[q, t] = leadh[t, 4 * q : 4 * q + 4, :]
    rd1[me_plane] = dst1[me_plane]
    d1_args = (16, me_plane, lambda q: dst1.at[q], lambda q: rd1.at[q], plane, d1, e1)
    send_all(*d1_args)
    split_half.wait_recv()
    for p in range(2):
        mine = mat[local[p], pl.ds(4 * k, 4)]
        half[pl.ds(4 * p, 4)] = jnp.where(o_k[p] == k, mine, rc1[p])

    def cross(d, w):
        source = half.at[(z + d) % 8, pl.ds(64 * (1 - xh) + 32 * w, 32), :]
        return remote(source, rx[w].at[d], sx.at[w, d], rxs.at[w, d], partner)

    def deal(d, w):
        return remote(stz[w].at[d], rc2[w].at[d], s2.at[w, d], r2.at[w, d], along((z + d) % 8))

    def scatter(d, w):
        zz = (z + d) % 8
        cross(d, w).wait_recv()
        own = jnp.where(zz < 4, o_xh[0], o_xh[1]) == xh
        value = jnp.where(own, half[zz, pl.ds(64 * xh + 32 * w, 32), :], rx[w][d])
        if d == 0:
            rc2[w][0] = value
        else:
            stz[w][d] = value
            deal(d, w).start()

    for w in waves:
        for d in FAR_FIRST + (0,):
            cross(d, w).start()

    first_col = 2 * ((xh * 8 + z) * 2 + k)
    first_row = 8 * me_row

    def find(n, carry):
        c = co[n] - first_col
        s = ro[n]
        out = []
        for l in range(2):
            out.append(carry[l] + jnp.where(c == l, s, 0))
        for l in range(2):
            out.append(carry[2 + l] + jnp.where(c == l, n, 0))
        for i in range(8):
            out.append(carry[4 + i] + jnp.where(s - first_row == i, n, 0))
        return tuple(out)

    found = lax.fori_loop(0, NODES, find, (jnp.int32(0),) * 12)
    slots = [n % NODES for n in found[:2]]
    col_node = [n % NODES for n in found[2:4]]
    row_node = [n % NODES for n in found[4:]]
    keep_row = [[pat[p, n] == 1 for n in row_node] for p in range(2)]

    for d in FAR_FIRST + (0,):
        scatter(d, 0)
    recv_all(*d1_args)
    for t, (p, n) in enumerate(lead):
        slot = ro[n] // 8
        pd1[t] = rd1[(o_xh[p] * 2 + slot // 4) * 4 + slot % 4, t]
    rd2[z] = pd1[...]
    d2_args = (8, z, lambda q: pd1, lambda q: rd2.at[q], along, d2, e2)
    send_all(*d2_args)
    for d in FAR_FIRST + (0,):
        scatter(d, 1)

    def spread(d, w):
        return remote(pc2[w], za[w].at[d], s4.at[w, d], r4.at[w, d], along((z + d) % 8))

    def hand_over(d, w):
        return remote(za[w].at[d], xa[w].at[d], s4x.at[w, d], r4x.at[w, d], partner)

    def start_gather(w):
        for d in FAR_FIRST:
            deal(d, w).wait_recv()
        piece = rc2[w][(z + 8 - jnp.where(z < 4, o_z[0], o_z[1])) % 8]
        pc2[w][...] = piece
        za[w][0] = piece
        for d in FAR_FIRST:
            spread(d, w).start()
        hand_over(0, w).start()

    start_gather(0)
    recv_all(*d2_args)
    for t, (p, n) in enumerate(lead):
        diag[k, me_plane, t] = rd2[o_z[p], t]
    d3_args = (16, me_plane, lambda q: diag.at[k, me_plane], lambda q: diag.at[k, q], plane, d3, e3)
    send_all(*d3_args)
    start_gather(1)

    def join(src, dst, i, w):
        return remote(src[w], dst[w], s5.at[i, w], r5.at[i, w], sib)

    for d in FAR_FIRST:
        spread(d, 0).wait_recv()
        hand_over(d, 0).start()
    join(za, zb, 0, 0).start()
    recv_all(*d3_args)
    remote(diag.at[k], diag.at[k], d4, e4, sib).start()
    for d in FAR_FIRST:
        spread(d, 1).wait_recv()
        hand_over(d, 1).start()
    join(za, zb, 0, 1).start()
    joined_lead = remote(diag.at[k], diag.at[1 - k], d4, e4, sib)
    joined_lead.wait_recv()

    rid = lax.broadcasted_iota(jnp.int32, (W, W), 0)
    cid = lax.broadcasted_iota(jnp.int32, (W, W), 1)
    eye = jnp.where(rid == cid, 1.0, 0.0).astype(F32)
    place_lead(diag, 0, wa)
    wb[...] = eye
    factor(wa, wb, 0, 6)

    def crossed(w):
        for d in range(8):
            hand_over(d, w).wait_recv()
        join(xa, xb, 1, w).start()

    def c1_args(w):
        return 8, me_row, lambda q: cst[w].at[q], lambda q: rc3[w].at[q], row_of, s6.at[w], r6.at[w]

    def c2_args(w):
        return 8, me_row, lambda q: pc3[w], lambda q: cbuf[w].at[q], row_of, s7.at[w], r7.at[w]

    def start_columns(w):
        join(za, zb, 0, w).wait_recv()
        join(xa, xb, 1, w).wait_recv()
        for p in range(2):
            for l in range(2):
                i = slots[l] % 8
                d = (z + 8 - 4 * p - i % 4) % 8
                mine = i // 4 == k
                cst[w][4 * p + 2 * l + xh] = jnp.where(mine, za[w][d], zb[w][d])
                cst[w][4 * p + 2 * l + 1 - xh] = jnp.where(mine, xa[w][d], xb[w][d])
        rc3[w][me_row] = cst[w][me_row]
        send_all(*c1_args(w))

    def pass_columns(w):
        recv_all(*c1_args(w))
        piece = rc3[w][jnp.where((me_row // 2) % 2 == 0, slots[0] // 8, slots[1] // 8)]
        pc3[w][...] = piece
        cbuf[w][me_row] = piece
        send_all(*c2_args(w))

    crossed(0)
    factor(wa, wb, 6, 9)
    crossed(1)
    start_columns(0)
    factor(wa, wb, 9, 12)
    start_columns(1)
    factor(wa, wb, 12, 16)
    low[0] = jnp.where(rid <= cid, wa[...], 0.0).T
    inv0 = wb[...]
    inv[0] = inv0
    place_lead(diag, 1, tile_a)
    f01 = nt(tile_a[...], inv0)
    f01_out[...] = f01
    place_lead(diag, 2, wa)
    wa[...] = wa[...] - nt(f01, f01)
    wb[...] = eye
    factor(wa, wb, 0, 7)
    pass_columns(0)
    pass_columns(1)
    factor(wa, wb, 7, 16)
    low[1] = jnp.where(rid <= cid, wa[...], 0.0).T
    inv[1] = wb[...]

    for d in range(8):
        t = (z + 8 - d) % 8
        for w in waves:
            for core, pieces in ((k, (za, xa)), (1 - k, (zb, xb))):
                rows[t // 4, 4 * core + t % 4, pl.ds(64 * xh + 32 * w, 32), :] = pieces[0][w][d]
                rows[t // 4, 4 * core + t % 4, pl.ds(64 * (1 - xh) + 32 * w, 32), :] = pieces[1][w][d]

    def mask(value, keeps):
        return jnp.concatenate(
            [jnp.where(keep, value[W * i : W * i + W], 0.0) for i, keep in enumerate(keeps)], axis=0
        )

    f0[...] = mask(nt3(rows[0].reshape(8 * W, W), inv[0]), keep_row[0])
    fh[:, :W], fl[:, :W] = parts(f0[...])
    f1 = mask(nt3(rows[1].reshape(8 * W, W) - nt3(f0[...], f01_out[...]), inv[1]), keep_row[1])
    fh[:, W:], fl[:, W:] = parts(f1)
    for l in range(2):
        first = col_node[l] == 0
        second = col_node[l] == 1
        for s in range(8):
            rows_s = slice(W * s, W * s + W)
            here = ((first & keep_row[0][s]), (second & keep_row[1][s]))
            edge = ((first & (row_node[s] == 0)), (second & (row_node[s] == 1)))
            tile = mat[l, s]
            tile = jnp.where(here[0], f0[rows_s], tile)
            tile = jnp.where(here[1], f1[rows_s], tile)
            tile = jnp.where(edge[0], low[0], tile)
            base[l, s] = jnp.where(edge[1], low[1], tile)
            fixed = here[0] | here[1] | edge[0] | edge[1]
            change = (row_node[s] >= col_node[l]) & jnp.logical_not(fixed)
            i = 8 * l + s
            info[i : i + 1, :] = jnp.where(change, jnp.ones((1, W), F32), 0.0)
    for p in range(2):
        for l in range(2):
            i = 16 + 2 * p + l
            info[i : i + 1, :] = jnp.where(pat[p, col_node[l]] == 1, jnp.ones((1, W), F32), 0.0)
    info[20:, :] = jnp.zeros((4, W), F32)
    for arguments in (d1_args, d2_args, d3_args, c1_args(0), c1_args(1), c2_args(0), c2_args(1)):
        sent_all(*arguments)
    for w in waves:
        for d in range(8):
            cross(d, w).wait_send()
            hand_over(d, w).wait_send()
            if d:
                deal(d, w).wait_send()
                spread(d, w).wait_send()
        join(za, zb, 0, w).wait_send()
        join(xa, xb, 1, w).wait_send()
    for copy in (split_lead, split_half, joined_lead):
        copy.wait_send()
    for w in waves:
        recv_all(*c2_args(w))
        for q in range(8):
            cols[q, 32 * w : 32 * w + 32, :] = cbuf[w][q]


def gather_tiles(mat, co, ro, pat):
    vmem = pl.BlockSpec(memory_space=pltpu.VMEM)
    hbm = pl.BlockSpec(memory_space=pltpu.HBM)
    dma = pltpu.SemaphoreType.DMA
    vm = lambda *shape: pltpu.VMEM(shape, F32)
    pair = lambda n: [dma((n,)), dma((n,))]
    pairs = lambda n: [dma((2, n)), dma((2, n))]
    out = lambda *shape, dtype=F32: jax.ShapeDtypeStruct(shape, dtype)
    return pl.pallas_call(
        comm_kernel,
        out_shape=(
            out(2, 8, W, W),
            out(8 * W, 2 * W, dtype=jnp.bfloat16),
            out(8 * W, 2 * W, dtype=jnp.bfloat16),
            out(2, W, W),
            out(W, W),
            out(8, 64, W),
            out(24, W),
        ),
        in_specs=[hbm] * 4,
        out_specs=(vmem,) * 7,
        scratch_shapes=[
            vm(2, 8, W, W),
            pltpu.SMEM((NODES,), jnp.int32),
            pltpu.SMEM((NODES,), jnp.int32),
            pltpu.SMEM((2, NODES), jnp.int32),
            vm(2, 4, W, W), vm(2, 4, W, W),
            vm(3, 64, W), vm(3, 64, W),
            vm(8, W, W), vm(3, 64, W), vm(2, 8, W, W),
            *[vm(8, 32, W)] * 6, *[vm(32, W)] * 2, *[vm(8, 32, W)] * 8,
            *[vm(8, 32, W)] * 4, *[vm(32, W)] * 2, *[vm(8, 32, W)] * 2,
            vm(16, 3, 4, W), vm(16, 3, 4, W), vm(3, 4, W), vm(8, 3, 4, W), vm(2, 16, 3, 4, W),
            vm(W, W), vm(W, W), vm(W, W), vm(2, W, W), vm(8 * W, W),
            dma((4,)),
            *pair(2), *pairs(8), *pairs(8), *pairs(8), *pairs(8), *pairs(2), *pairs(8), *pairs(8),
            *pair(16), *pair(8), *pair(16), dma, dma,
        ],
        compiler_params=pltpu.CompilerParams(
            collective_id=0, has_side_effects=True, vmem_limit_bytes=40 * 1024 * 1024
        ),
        name="gather_tiles",
    )(mat, co, ro, pat)


def lanes(x):
    return jnp.broadcast_to(x, (x.shape[0], W))


def subs(x):
    return jnp.broadcast_to(x, (8, W))


def factor(wa_ref, wb_ref, first, last):
    rid = lax.broadcasted_iota(jnp.int32, (8, W), 0)
    for c in range(8 * first, 8 * last, 8):
        wa = wa_ref[c : c + 8, :]
        wb = wb_ref[c : c + 8, :]
        cl = [lanes(wa[:, c + i : c + i + 1]) for i in range(8)]
        pa, pb, sc, lt = [], [], [], []
        for i in range(8):
            s = lax.rsqrt(subs(cl[i][i : i + 1]))
            li = cl[i] * s
            ra = subs(wa[i : i + 1]) * s
            rb = subs(wb[i : i + 1]) * s
            low = jnp.where(rid > i, li, 0.0)
            wa = jnp.where(rid == i, ra, wa - low * ra)
            wb = jnp.where(rid == i, rb, wb - low * rb)
            row = {}
            for j in range(i + 1, 8):
                row[j] = subs(li[j : j + 1])
                cl[j] = cl[j] - li * row[j]
            pa.append(ra)
            pb.append(rb)
            sc.append(s)
            lt.append(row)
        wa_ref[c : c + 8, :] = wa
        wb_ref[c : c + 8, :] = wb
        g = c + 8
        while g < W:
            size = min(16, W - g)
            tile = lambda v: jnp.concatenate([v] * (size // 8), axis=0) if size > 8 else v
            ga = wa_ref[g : g + size, :]
            gb = wb_ref[g : g + size, :]
            gc = [lanes(ga[:, c + i : c + i + 1]) for i in range(8)]
            for i in range(8):
                li = gc[i] * tile(sc[i])
                ga = ga - li * tile(pa[i])
                gb = gb - li * tile(pb[i])
                for j in range(i + 1, 8):
                    gc[j] = gc[j] - li * tile(lt[i][j])
            wa_ref[g : g + size, :] = ga
            wb_ref[g : g + size, :] = gb
            g += size


def nt(a, b):
    return lax.dot_general(a, b, (((1,), (1,)), ((), ())), precision=PRECISE, preferred_element_type=F32)


def nt16(a, b):
    return lax.dot_general(a, b, (((1,), (1,)), ((), ())), preferred_element_type=F32)


def parts(a):
    high = a.astype(jnp.bfloat16)
    return high, (a - high.astype(F32)).astype(jnp.bfloat16)


def nt3(a, b):
    ah, al = parts(a)
    bh, bl = parts(b)
    both = nt16(jnp.concatenate([ah, al], axis=1), jnp.concatenate([bh, bh], axis=1))
    return both + nt16(ah, bl)


def apply_kernel(base, fh, fl, inv, f01, cols, info, out, buf, sem):
    def flag(i):
        return info[i : i + 1, :] > 0.5

    def mask(value, p):
        return jnp.concatenate(
            [jnp.where(flag(16 + 2 * p + l), value[W * l : W * l + W], 0.0) for l in range(2)], axis=0
        )

    raw = lambda p: cols[4 * p : 4 * p + 4].reshape(2 * W, W)
    g0 = mask(nt3(raw(0), inv[0]), 0)
    g1 = mask(nt3(raw(1) - nt3(g0, f01[...]), inv[1]), 1)
    g0h, g0l = parts(g0)
    g1h, g1l = parts(g1)
    gh = jnp.concatenate([g0h, g1h], axis=1)
    gl = jnp.concatenate([g0l, g1l], axis=1)
    copies = []
    for s in range(0, 8, 2):
        both = slice(W * s, W * s + 2 * W)
        step = nt16(fh[both], gh) + nt16(fl[both], gh) + nt16(fh[both], gl)
        for l in range(2):
            for i in range(2):
                old = base[l, s + i]
                new = old - step[W * i : W * i + W, W * l : W * l + W]
                buf[l, s + i] = jnp.where(flag(8 * l + s + i), new, old)
            copy = pltpu.make_async_copy(buf.at[l, pl.ds(s, 2)], out.at[l, pl.ds(s, 2)], sem.at[l + s])
            copy.start()
            copies.append(copy)
    for copy in copies:
        copy.wait()


def apply_panels(base, fh, fl, inv, f01, cols, info):
    vmem = pl.BlockSpec(memory_space=pltpu.VMEM)
    return pl.pallas_call(
        apply_kernel,
        out_shape=jax.ShapeDtypeStruct((2, 8, W, W), F32),
        in_specs=[vmem] * 7,
        out_specs=pl.BlockSpec(memory_space=pltpu.HBM),
        scratch_shapes=[pltpu.VMEM((2, 8, W, W), F32), pltpu.SemaphoreType.DMA((8,))],
        compiler_params=pltpu.CompilerParams(vmem_limit_bytes=16 * 1024 * 1024),
        name="apply_panels",
    )(base, fh, fl, inv, f01, cols, info)


def body(matrix, col_owner, row_owner, pattern):
    held = [pltpu.with_memory_space_constraint(x, pltpu.HBM) for x in (matrix, col_owner, row_owner, pattern)]
    return apply_panels(*gather_tiles(*held))


def solution(mesh):
    return jax.shard_map(
        body,
        mesh=mesh,
        in_specs=(P("col", "row", None, None), P(), P(), P()),
        out_specs=P("col", "row", None, None),
        check_vma=False,
    )
```

```python
import functools

import jax
import jax.numpy as jnp
from jax import lax
from jax.experimental import pallas as pl
from jax.experimental.pallas import tpu as pltpu
from jax.sharding import PartitionSpec as P

MESH = pl.DeviceIdType.MESH
F32 = jnp.float32
PRECISE = lax.Precision.HIGHEST
W = 128
NODES = 64


def my_place():
    col = lax.axis_index("col")
    row = lax.axis_index("row")
    return col // 16, (col // 2) % 8, col % 2, row // 4, row % 4


def device(xh, z, k, xl, y):
    return {"col": (xh * 8 + z) * 2 + k, "row": xl * 4 + y}


def send_all(count, me, source, slot, target, send_sem, recv_sem):
    def step(i, carry):
        q = (me + i) % count
        pltpu.make_async_remote_copy(
            src_ref=source(q),
            dst_ref=slot(me),
            send_sem=send_sem.at[q],
            recv_sem=recv_sem.at[me],
            device_id=target(q),
            device_id_type=MESH,
        ).start()
        return carry

    lax.fori_loop(1, count, step, 0)


def wait_all(count, me, source, slot, target, send_sem, recv_sem, sent=False):
    def step(q, carry):
        @pl.when(q != me)
        def _():
            copy = pltpu.make_async_remote_copy(
                src_ref=source(q),
                dst_ref=slot(q),
                send_sem=send_sem.at[q],
                recv_sem=recv_sem.at[q],
                device_id=target(q),
                device_id_type=MESH,
            )
            if sent:
                copy.wait_send()
            else:
                copy.wait_recv()

        return carry

    lax.fori_loop(0, count, step, 0)


def recv_all(*args):
    wait_all(*args)


def sent_all(*args):
    wait_all(*args, sent=True)


def place_lead(diag, t, dst):
    for k in range(2):
        for q in range(16):
            dst[64 * k + 4 * q : 64 * k + 4 * q + 4, :] = diag[k, q, t]


FAR_FIRST = (4, 3, 5, 2, 6, 1, 7)


def comm_kernel(
    mat_hbm, co_hbm, ro_hbm, pat_hbm, base, fh, fl, inv, f01_out, cols, info,
    mat, co, ro, pat, st1, rc1, stl, rcl, half, leadh, rows,
    rx0, rx1, stz0, stz1, rc20, rc21, pc20, pc21, za0, za1, xa0, xa1, zb0, zb1, xb0, xb1,
    cst0, cst1, rc30, rc31, pc30, pc31, cbuf0, cbuf1,
    dst1, rd1, pd1, rd2, diag, wa, wb, tile_a, low, f0,
    ld, s1, r1, sx, rxs, s2, r2, s4, r4, s4x, r4x, s5, r5, s6, r6, s7, r7,
    d1, e1, d2, e2, d3, e3, d4, e4,
):
    rx, stz, rc2, pc2 = (rx0, rx1), (stz0, stz1), (rc20, rc21), (pc20, pc21)
    za, xa, zb, xb = (za0, za1), (xa0, xa1), (zb0, zb1), (xb0, xb1)
    cst, rc3, pc3, cbuf = (cst0, cst1), (rc30, rc31), (pc30, pc31), (cbuf0, cbuf1)
    waves = (0, 1)
    xh, z, k, xl, y = my_place()
    me_plane = (xh * 2 + xl) * 4 + y
    me_row = xl * 4 + y

    def plane(q):
        return device(q // 8, z, k, (q // 4) % 2, q % 4)

    def along(q):
        return device(xh, q, k, xl, y)

    def row_of(q):
        return device(xh, z, k, q // 4, q % 4)

    sib = device(xh, z, 1 - k, xl, y)
    partner = device(1 - xh, z, k, xl, y)

    def remote(src, dst, send, recv, target):
        return pltpu.make_async_remote_copy(
            src_ref=src, dst_ref=dst, send_sem=send, recv_sem=recv, device_id=target, device_id_type=MESH
        )

    loads = [
        pltpu.make_async_copy(src, dst, ld.at[i])
        for i, (src, dst) in enumerate(((co_hbm, co), (ro_hbm, ro), (pat_hbm, pat), (mat_hbm, mat)))
    ]
    for copy in loads:
        copy.start()

    barrier = pltpu.get_barrier_semaphore()

    def greet(count, me, target):
        def step(q, carry):
            @pl.when(q != me)
            def _():
                pl.semaphore_signal(barrier, inc=1, device_id=target(q), device_id_type=MESH)

            return carry

        lax.fori_loop(0, count, step, 0)

    greet(16, me_plane, plane)
    greet(8, z, along)
    pl.semaphore_signal(barrier, inc=1, device_id=sib, device_id_type=MESH)
    for copy in loads:
        copy.wait()

    owner = [co[p] // 2 for p in range(2)]
    local = [co[p] % 2 for p in range(2)]
    o_xh = [o // 16 for o in owner]
    o_z = [(o // 2) % 8 for o in owner]
    o_k = [o % 2 for o in owner]
    lead = ((0, 0), (0, 1), (1, 1))
    for p in range(2):
        st1[p] = mat[local[p], pl.ds(4 * (1 - k), 4)]
    for t, (p, n) in enumerate(lead):
        stl[t] = mat[local[p], ro[n] % 8, pl.ds(64 * (1 - k), 64), :]

    pl.semaphore_wait(barrier, 15 + 7 + 1)

    split_lead = remote(stl, rcl, s1.at[0], r1.at[0], sib)
    split_half = remote(st1, rc1, s1.at[1], r1.at[1], sib)
    split_lead.start()
    split_half.start()
    split_lead.wait_recv()
    for t, (p, n) in enumerate(lead):
        mine = mat[local[p], ro[n] % 8, pl.ds(64 * k, 64), :]
        leadh[t] = jnp.where(o_k[p] == k, mine, rcl[t])
        for q in range(16):
            dst1[q, t] = leadh[t, 4 * q : 4 * q + 4, :]
    rd1[me_plane] = dst1[me_plane]
    d1_args = (16, me_plane, lambda q: dst1.at[q], lambda q: rd1.at[q], plane, d1, e1)
    send_all(*d1_args)
    split_half.wait_recv()
    for p in range(2):
        mine = mat[local[p], pl.ds(4 * k, 4)]
        half[pl.ds(4 * p, 4)] = jnp.where(o_k[p] == k, mine, rc1[p])

    def cross(d, w):
        source = half.at[(z + d) % 8, pl.ds(64 * (1 - xh) + 32 * w, 32), :]
        return remote(source, rx[w].at[d], sx.at[w, d], rxs.at[w, d], partner)

    def deal(d, w):
        return remote(stz[w].at[d], rc2[w].at[d], s2.at[w, d], r2.at[w, d], along((z + d) % 8))

    def scatter(d, w):
        zz = (z + d) % 8
        cross(d, w).wait_recv()
        own = jnp.where(zz < 4, o_xh[0], o_xh[1]) == xh
        value = jnp.where(own, half[zz, pl.ds(64 * xh + 32 * w, 32), :], rx[w][d])
        if d == 0:
            rc2[w][0] = value
        else:
            stz[w][d] = value
            deal(d, w).start()

    for w in waves:
        for d in FAR_FIRST + (0,):
            cross(d, w).start()

    first_col = 2 * ((xh * 8 + z) * 2 + k)
    first_row = 8 * me_row

    def find(n, carry):
        c = co[n] - first_col
        s = ro[n]
        out = []
        for l in range(2):
            out.append(carry[l] + jnp.where(c == l, s, 0))
        for l in range(2):
            out.append(carry[2 + l] + jnp.where(c == l, n, 0))
        for i in range(8):
            out.append(carry[4 + i] + jnp.where(s - first_row == i, n, 0))
        return tuple(out)

    found = lax.fori_loop(0, NODES, find, (jnp.int32(0),) * 12)
    slots = [n % NODES for n in found[:2]]
    col_node = [n % NODES for n in found[2:4]]
    row_node = [n % NODES for n in found[4:]]
    keep_row = [[pat[p, n] == 1 for n in row_node] for p in range(2)]

    for d in FAR_FIRST[:4]:
        scatter(d, 0)
    recv_all(*d1_args)
    for t, (p, n) in enumerate(lead):
        slot = ro[n] // 8
        pd1[t] = rd1[(o_xh[p] * 2 + slot // 4) * 4 + slot % 4, t]
    rd2[z] = pd1[...]
    d2_args = (8, z, lambda q: pd1, lambda q: rd2.at[q], along, d2, e2)
    send_all(*d2_args)
    for d in FAR_FIRST[4:] + (0,):
        scatter(d, 0)
    for d in FAR_FIRST + (0,):
        scatter(d, 1)

    def spread(d, w):
        return remote(pc2[w], za[w].at[d], s4.at[w, d], r4.at[w, d], along((z + d) % 8))

    def hand_over(d, w):
        return remote(za[w].at[d], xa[w].at[d], s4x.at[w, d], r4x.at[w, d], partner)

    def start_gather(w):
        for d in FAR_FIRST:
            deal(d, w).wait_recv()
        piece = rc2[w][(z + 8 - jnp.where(z < 4, o_z[0], o_z[1])) % 8]
        pc2[w][...] = piece
        za[w][0] = piece
        for d in FAR_FIRST:
            spread(d, w).start()
        hand_over(0, w).start()

    start_gather(0)
    recv_all(*d2_args)
    for t, (p, n) in enumerate(lead):
        diag[k, me_plane, t] = rd2[o_z[p], t]
    d3_args = (16, me_plane, lambda q: diag.at[k, me_plane], lambda q: diag.at[k, q], plane, d3, e3)
    send_all(*d3_args)
    start_gather(1)

    def join(src, dst, i, w):
        return remote(src[w], dst[w], s5.at[i, w], r5.at[i, w], sib)

    for d in FAR_FIRST:
        spread(d, 0).wait_recv()
        hand_over(d, 0).start()
    join(za, zb, 0, 0).start()
    recv_all(*d3_args)
    remote(diag.at[k], diag.at[k], d4, e4, sib).start()
    for d in FAR_FIRST:
        spread(d, 1).wait_recv()
        hand_over(d, 1).start()
    join(za, zb, 0, 1).start()
    joined_lead = remote(diag.at[k], diag.at[1 - k], d4, e4, sib)
    joined_lead.wait_recv()

    rid = lax.broadcasted_iota(jnp.int32, (W, W), 0)
    cid = lax.broadcasted_iota(jnp.int32, (W, W), 1)
    eye = jnp.where(rid == cid, 1.0, 0.0).astype(F32)
    place_lead(diag, 0, wa)
    wb[...] = eye
    factor(wa, wb, 0, 6)

    def crossed(w):
        for d in range(8):
            hand_over(d, w).wait_recv()
        join(xa, xb, 1, w).start()

    def c1_args(w):
        return 8, me_row, lambda q: cst[w].at[q], lambda q: rc3[w].at[q], row_of, s6.at[w], r6.at[w]

    def c2_args(w):
        return 8, me_row, lambda q: pc3[w], lambda q: cbuf[w].at[q], row_of, s7.at[w], r7.at[w]

    def start_columns(w):
        join(za, zb, 0, w).wait_recv()
        join(xa, xb, 1, w).wait_recv()
        for p in range(2):
            for l in range(2):
                i = slots[l] % 8
                d = (z + 8 - 4 * p - i % 4) % 8
                mine = i // 4 == k
                cst[w][4 * p + 2 * l + xh] = jnp.where(mine, za[w][d], zb[w][d])
                cst[w][4 * p + 2 * l + 1 - xh] = jnp.where(mine, xa[w][d], xb[w][d])
        rc3[w][me_row] = cst[w][me_row]
        send_all(*c1_args(w))

    def pass_columns(w):
        recv_all(*c1_args(w))
        piece = rc3[w][jnp.where((me_row // 2) % 2 == 0, slots[0] // 8, slots[1] // 8)]
        pc3[w][...] = piece
        cbuf[w][me_row] = piece
        send_all(*c2_args(w))

    crossed(0)
    factor(wa, wb, 6, 9)
    crossed(1)
    start_columns(0)
    factor(wa, wb, 9, 12)
    start_columns(1)
    factor(wa, wb, 12, 16)
    low[0] = jnp.where(rid <= cid, wa[...], 0.0).T
    inv0 = wb[...]
    inv[0] = inv0
    place_lead(diag, 1, tile_a)
    f01 = nt(tile_a[...], inv0)
    f01_out[...] = f01
    place_lead(diag, 2, wa)
    wa[...] = wa[...] - nt(f01, f01)
    wb[...] = eye
    factor(wa, wb, 0, 7)
    pass_columns(0)
    pass_columns(1)
    factor(wa, wb, 7, 16)
    low[1] = jnp.where(rid <= cid, wa[...], 0.0).T
    inv[1] = wb[...]

    for d in range(8):
        t = (z + 8 - d) % 8
        for w in waves:
            for core, pieces in ((k, (za, xa)), (1 - k, (zb, xb))):
                rows[t // 4, 4 * core + t % 4, pl.ds(64 * xh + 32 * w, 32), :] = pieces[0][w][d]
                rows[t // 4, 4 * core + t % 4, pl.ds(64 * (1 - xh) + 32 * w, 32), :] = pieces[1][w][d]

    def mask(value, keeps):
        return jnp.concatenate(
            [jnp.where(keep, value[W * i : W * i + W], 0.0) for i, keep in enumerate(keeps)], axis=0
        )

    f0[...] = mask(nt3(rows[0].reshape(8 * W, W), inv[0]), keep_row[0])
    fh[:, :W], fl[:, :W] = parts(f0[...])
    f1 = mask(nt3(rows[1].reshape(8 * W, W) - nt3(f0[...], f01_out[...]), inv[1]), keep_row[1])
    fh[:, W:], fl[:, W:] = parts(f1)
    for l in range(2):
        first = col_node[l] == 0
        second = col_node[l] == 1
        for s in range(8):
            rows_s = slice(W * s, W * s + W)
            here = ((first & keep_row[0][s]), (second & keep_row[1][s]))
            edge = ((first & (row_node[s] == 0)), (second & (row_node[s] == 1)))
            tile = mat[l, s]
            tile = jnp.where(here[0], f0[rows_s], tile)
            tile = jnp.where(here[1], f1[rows_s], tile)
            tile = jnp.where(edge[0], low[0], tile)
            base[l, s] = jnp.where(edge[1], low[1], tile)
            fixed = here[0] | here[1] | edge[0] | edge[1]
            change = (row_node[s] >= col_node[l]) & jnp.logical_not(fixed)
            i = 8 * l + s
            info[i : i + 1, :] = jnp.where(change, jnp.ones((1, W), F32), 0.0)
    for p in range(2):
        for l in range(2):
            i = 16 + 2 * p + l
            info[i : i + 1, :] = jnp.where(pat[p, col_node[l]] == 1, jnp.ones((1, W), F32), 0.0)
    info[20:, :] = jnp.zeros((4, W), F32)
    for arguments in (d1_args, d2_args, d3_args, c1_args(0), c1_args(1), c2_args(0), c2_args(1)):
        sent_all(*arguments)
    for w in waves:
        for d in range(8):
            cross(d, w).wait_send()
            hand_over(d, w).wait_send()
            if d:
                deal(d, w).wait_send()
                spread(d, w).wait_send()
        join(za, zb, 0, w).wait_send()
        join(xa, xb, 1, w).wait_send()
    for copy in (split_lead, split_half, joined_lead):
        copy.wait_send()
    for w in waves:
        recv_all(*c2_args(w))
        for q in range(8):
            cols[q, 32 * w : 32 * w + 32, :] = cbuf[w][q]


def gather_tiles(mat, co, ro, pat):
    vmem = pl.BlockSpec(memory_space=pltpu.VMEM)
    hbm = pl.BlockSpec(memory_space=pltpu.HBM)
    dma = pltpu.SemaphoreType.DMA
    vm = lambda *shape: pltpu.VMEM(shape, F32)
    pair = lambda n: [dma((n,)), dma((n,))]
    pairs = lambda n: [dma((2, n)), dma((2, n))]
    out = lambda *shape, dtype=F32: jax.ShapeDtypeStruct(shape, dtype)
    return pl.pallas_call(
        comm_kernel,
        out_shape=(
            out(2, 8, W, W),
            out(8 * W, 2 * W, dtype=jnp.bfloat16),
            out(8 * W, 2 * W, dtype=jnp.bfloat16),
            out(2, W, W),
            out(W, W),
            out(8, 64, W),
            out(24, W),
        ),
        in_specs=[hbm] * 4,
        out_specs=(vmem,) * 7,
        scratch_shapes=[
            vm(2, 8, W, W),
            pltpu.SMEM((NODES,), jnp.int32),
            pltpu.SMEM((NODES,), jnp.int32),
            pltpu.SMEM((2, NODES), jnp.int32),
            vm(2, 4, W, W), vm(2, 4, W, W),
            vm(3, 64, W), vm(3, 64, W),
            vm(8, W, W), vm(3, 64, W), vm(2, 8, W, W),
            *[vm(8, 32, W)] * 6, *[vm(32, W)] * 2, *[vm(8, 32, W)] * 8,
            *[vm(8, 32, W)] * 4, *[vm(32, W)] * 2, *[vm(8, 32, W)] * 2,
            vm(16, 3, 4, W), vm(16, 3, 4, W), vm(3, 4, W), vm(8, 3, 4, W), vm(2, 16, 3, 4, W),
            vm(W, W), vm(W, W), vm(W, W), vm(2, W, W), vm(8 * W, W),
            dma((4,)),
            *pair(2), *pairs(8), *pairs(8), *pairs(8), *pairs(8), *pairs(2), *pairs(8), *pairs(8),
            *pair(16), *pair(8), *pair(16), dma, dma,
        ],
        compiler_params=pltpu.CompilerParams(
            collective_id=0, has_side_effects=True, vmem_limit_bytes=40 * 1024 * 1024
        ),
        name="gather_tiles",
    )(mat, co, ro, pat)


def lanes(x):
    return jnp.broadcast_to(x, (x.shape[0], W))


def subs(x):
    return jnp.broadcast_to(x, (8, W))


def factor(wa_ref, wb_ref, first, last):
    rid = lax.broadcasted_iota(jnp.int32, (8, W), 0)
    for c in range(8 * first, 8 * last, 8):
        wa = wa_ref[c : c + 8, :]
        wb = wb_ref[c : c + 8, :]
        cl = [lanes(wa[:, c + i : c + i + 1]) for i in range(8)]
        pa, pb, sc, lt = [], [], [], []
        for i in range(8):
            s = lax.rsqrt(subs(cl[i][i : i + 1]))
            li = cl[i] * s
            ra = subs(wa[i : i + 1]) * s
            rb = subs(wb[i : i + 1]) * s
            low = jnp.where(rid > i, li, 0.0)
            wa = jnp.where(rid == i, ra, wa - low * ra)
            wb = jnp.where(rid == i, rb, wb - low * rb)
            row = {}
            for j in range(i + 1, 8):
                row[j] = subs(li[j : j + 1])
                cl[j] = cl[j] - li * row[j]
            pa.append(ra)
            pb.append(rb)
            sc.append(s)
            lt.append(row)
        wa_ref[c : c + 8, :] = wa
        wb_ref[c : c + 8, :] = wb
        g = c + 8
        while g < W:
            size = min(16, W - g)
            tile = lambda v: jnp.concatenate([v] * (size // 8), axis=0) if size > 8 else v
            ga = wa_ref[g : g + size, :]
            gb = wb_ref[g : g + size, :]
            gc = [lanes(ga[:, c + i : c + i + 1]) for i in range(8)]
            for i in range(8):
                li = gc[i] * tile(sc[i])
                ga = ga - li * tile(pa[i])
                gb = gb - li * tile(pb[i])
                for j in range(i + 1, 8):
                    gc[j] = gc[j] - li * tile(lt[i][j])
            wa_ref[g : g + size, :] = ga
            wb_ref[g : g + size, :] = gb
            g += size


def nt(a, b):
    return lax.dot_general(a, b, (((1,), (1,)), ((), ())), precision=PRECISE, preferred_element_type=F32)


def nt16(a, b):
    return lax.dot_general(a, b, (((1,), (1,)), ((), ())), preferred_element_type=F32)


def parts(a):
    high = a.astype(jnp.bfloat16)
    return high, (a - high.astype(F32)).astype(jnp.bfloat16)


def nt3(a, b):
    ah, al = parts(a)
    bh, bl = parts(b)
    both = nt16(jnp.concatenate([ah, al], axis=1), jnp.concatenate([bh, bh], axis=1))
    return both + nt16(ah, bl)


def apply_kernel(base, fh, fl, inv, f01, cols, info, out, buf, sem):
    def flag(i):
        return info[i : i + 1, :] > 0.5

    def mask(value, p):
        return jnp.concatenate(
            [jnp.where(flag(16 + 2 * p + l), value[W * l : W * l + W], 0.0) for l in range(2)], axis=0
        )

    raw = lambda p: cols[4 * p : 4 * p + 4].reshape(2 * W, W)
    g0 = mask(nt3(raw(0), inv[0]), 0)
    g1 = mask(nt3(raw(1) - nt3(g0, f01[...]), inv[1]), 1)
    g0h, g0l = parts(g0)
    g1h, g1l = parts(g1)
    gh = jnp.concatenate([g0h, g1h], axis=1)
    gl = jnp.concatenate([g0l, g1l], axis=1)
    copies = []
    for s in range(0, 8, 2):
        both = slice(W * s, W * s + 2 * W)
        step = nt16(fh[both], gh) + nt16(fl[both], gh) + nt16(fh[both], gl)
        for l in range(2):
            for i in range(2):
                old = base[l, s + i]
                new = old - step[W * i : W * i + W, W * l : W * l + W]
                buf[l, s + i] = jnp.where(flag(8 * l + s + i), new, old)
            copy = pltpu.make_async_copy(buf.at[l, pl.ds(s, 2)], out.at[l, pl.ds(s, 2)], sem.at[l + s])
            copy.start()
            copies.append(copy)
    for copy in copies:
        copy.wait()


def apply_panels(base, fh, fl, inv, f01, cols, info):
    vmem = pl.BlockSpec(memory_space=pltpu.VMEM)
    return pl.pallas_call(
        apply_kernel,
        out_shape=jax.ShapeDtypeStruct((2, 8, W, W), F32),
        in_specs=[vmem] * 7,
        out_specs=pl.BlockSpec(memory_space=pltpu.HBM),
        scratch_shapes=[pltpu.VMEM((2, 8, W, W), F32), pltpu.SemaphoreType.DMA((8,))],
        compiler_params=pltpu.CompilerParams(vmem_limit_bytes=16 * 1024 * 1024),
        name="apply_panels",
    )(base, fh, fl, inv, f01, cols, info)


def body(matrix, col_owner, row_owner, pattern):
    held = [pltpu.with_memory_space_constraint(x, pltpu.HBM) for x in (matrix, col_owner, row_owner, pattern)]
    return apply_panels(*gather_tiles(*held))


def solution(mesh):
    return jax.shard_map(
        body,
        mesh=mesh,
        in_specs=(P("col", "row", None, None), P(), P(), P()),
        out_specs=P("col", "row", None, None),
        check_vma=False,
    )
```

```python
import functools

import jax
import jax.numpy as jnp
from jax import lax
from jax.experimental import pallas as pl
from jax.experimental.pallas import tpu as pltpu
from jax.sharding import PartitionSpec as P

MESH = pl.DeviceIdType.MESH
F32 = jnp.float32
PRECISE = lax.Precision.HIGHEST
W = 128
NODES = 64


def my_place():
    col = lax.axis_index("col")
    row = lax.axis_index("row")
    return col // 16, (col // 2) % 8, col % 2, row // 4, row % 4


def device(xh, z, k, xl, y):
    return {"col": (xh * 8 + z) * 2 + k, "row": xl * 4 + y}


def send_all(count, me, source, slot, target, send_sem, recv_sem):
    def step(i, carry):
        q = (me + i) % count
        pltpu.make_async_remote_copy(
            src_ref=source(q),
            dst_ref=slot(me),
            send_sem=send_sem.at[q],
            recv_sem=recv_sem.at[me],
            device_id=target(q),
            device_id_type=MESH,
        ).start()
        return carry

    lax.fori_loop(1, count, step, 0)


def wait_all(count, me, source, slot, target, send_sem, recv_sem, sent=False):
    def step(q, carry):
        @pl.when(q != me)
        def _():
            copy = pltpu.make_async_remote_copy(
                src_ref=source(q),
                dst_ref=slot(q),
                send_sem=send_sem.at[q],
                recv_sem=recv_sem.at[q],
                device_id=target(q),
                device_id_type=MESH,
            )
            if sent:
                copy.wait_send()
            else:
                copy.wait_recv()

        return carry

    lax.fori_loop(0, count, step, 0)


def recv_all(*args):
    wait_all(*args)


def sent_all(*args):
    wait_all(*args, sent=True)


def place_lead(diag, t, dst):
    for k in range(2):
        for q in range(16):
            dst[64 * k + 4 * q : 64 * k + 4 * q + 4, :] = diag[k, q, t]


FAR_FIRST = (4, 3, 5, 2, 6, 1, 7)


def comm_kernel(
    mat_hbm, co_hbm, ro_hbm, pat_hbm, base, fh, fl, inv, f01_out, cols, info,
    mat, co, ro, pat, st1, rc1, stl, rcl, half, leadh, rows,
    rx0, rx1, stz0, stz1, rc20, rc21, pc20, pc21, za0, za1, xa0, xa1, zb0, zb1, xb0, xb1,
    cst0, cst1, rc30, rc31, pc30, pc31, cbuf0, cbuf1,
    dst1, rd1, pd1, rd2, diag, wa, wb, tile_a, low, f0,
    ld, s1, r1, sx, rxs, s2, r2, s4, r4, s4x, r4x, s5, r5, s6, r6, s7, r7,
    d1, e1, d2, e2, d3, e3, d4, e4,
):
    rx, stz, rc2, pc2 = (rx0, rx1), (stz0, stz1), (rc20, rc21), (pc20, pc21)
    za, xa, zb, xb = (za0, za1), (xa0, xa1), (zb0, zb1), (xb0, xb1)
    cst, rc3, pc3, cbuf = (cst0, cst1), (rc30, rc31), (pc30, pc31), (cbuf0, cbuf1)
    waves = (0, 1)
    xh, z, k, xl, y = my_place()
    me_plane = (xh * 2 + xl) * 4 + y
    me_row = xl * 4 + y

    def plane(q):
        return device(q // 8, z, k, (q // 4) % 2, q % 4)

    def along(q):
        return device(xh, q, k, xl, y)

    def row_of(q):
        return device(xh, z, k, q // 4, q % 4)

    sib = device(xh, z, 1 - k, xl, y)
    partner = device(1 - xh, z, k, xl, y)

    def remote(src, dst, send, recv, target):
        return pltpu.make_async_remote_copy(
            src_ref=src, dst_ref=dst, send_sem=send, recv_sem=recv, device_id=target, device_id_type=MESH
        )

    loads = [
        pltpu.make_async_copy(src, dst, ld.at[i])
        for i, (src, dst) in enumerate(((co_hbm, co), (ro_hbm, ro), (pat_hbm, pat), (mat_hbm, mat)))
    ]
    for copy in loads:
        copy.start()

    barrier = pltpu.get_barrier_semaphore()

    def greet(count, me, target):
        def step(q, carry):
            @pl.when(q != me)
            def _():
                pl.semaphore_signal(barrier, inc=1, device_id=target(q), device_id_type=MESH)

            return carry

        lax.fori_loop(0, count, step, 0)

    greet(16, me_plane, plane)
    greet(8, z, along)
    pl.semaphore_signal(barrier, inc=1, device_id=sib, device_id_type=MESH)
    for copy in loads:
        copy.wait()

    owner = [co[p] // 2 for p in range(2)]
    local = [co[p] % 2 for p in range(2)]
    o_xh = [o // 16 for o in owner]
    o_z = [(o // 2) % 8 for o in owner]
    o_k = [o % 2 for o in owner]
    lead = ((0, 0), (0, 1), (1, 1))
    for p in range(2):
        st1[p] = mat[local[p], pl.ds(4 * (1 - k), 4)]
    for t, (p, n) in enumerate(lead):
        stl[t] = mat[local[p], ro[n] % 8, pl.ds(64 * (1 - k), 64), :]

    pl.semaphore_wait(barrier, 15 + 7 + 1)

    split_lead = remote(stl, rcl, s1.at[0], r1.at[0], sib)
    split_half = remote(st1, rc1, s1.at[1], r1.at[1], sib)
    split_lead.start()
    split_half.start()
    split_lead.wait_recv()
    for t, (p, n) in enumerate(lead):
        mine = mat[local[p], ro[n] % 8, pl.ds(64 * k, 64), :]
        leadh[t] = jnp.where(o_k[p] == k, mine, rcl[t])
        for q in range(16):
            dst1[q, t] = leadh[t, 4 * q : 4 * q + 4, :]
    rd1[me_plane] = dst1[me_plane]
    d1_args = (16, me_plane, lambda q: dst1.at[q], lambda q: rd1.at[q], plane, d1, e1)
    send_all(*d1_args)
    split_half.wait_recv()
    for p in range(2):
        mine = mat[local[p], pl.ds(4 * k, 4)]
        half[pl.ds(4 * p, 4)] = jnp.where(o_k[p] == k, mine, rc1[p])

    def cross(d, w):
        source = half.at[(z + d) % 8, pl.ds(64 * (1 - xh) + 32 * w, 32), :]
        return remote(source, rx[w].at[d], sx.at[w, d], rxs.at[w, d], partner)

    def deal(d, w):
        return remote(stz[w].at[d], rc2[w].at[d], s2.at[w, d], r2.at[w, d], along((z + d) % 8))

    def scatter(d, w):
        zz = (z + d) % 8
        cross(d, w).wait_recv()
        own = jnp.where(zz < 4, o_xh[0], o_xh[1]) == xh
        value = jnp.where(own, half[zz, pl.ds(64 * xh + 32 * w, 32), :], rx[w][d])
        if d == 0:
            rc2[w][0] = value
        else:
            stz[w][d] = value
            deal(d, w).start()

    for w in waves:
        for d in FAR_FIRST + (0,):
            cross(d, w).start()

    first_col = 2 * ((xh * 8 + z) * 2 + k)
    first_row = 8 * me_row

    def find(n, carry):
        c = co[n] - first_col
        s = ro[n]
        out = []
        for l in range(2):
            out.append(carry[l] + jnp.where(c == l, s, 0))
        for l in range(2):
            out.append(carry[2 + l] + jnp.where(c == l, n, 0))
        for i in range(8):
            out.append(carry[4 + i] + jnp.where(s - first_row == i, n, 0))
        return tuple(out)

    found = lax.fori_loop(0, NODES, find, (jnp.int32(0),) * 12)
    slots = [n % NODES for n in found[:2]]
    col_node = [n % NODES for n in found[2:4]]
    row_node = [n % NODES for n in found[4:]]
    keep_row = [[pat[p, n] == 1 for n in row_node] for p in range(2)]

    for d in FAR_FIRST[:4]:
        scatter(d, 0)
    recv_all(*d1_args)
    for t, (p, n) in enumerate(lead):
        slot = ro[n] // 8
        pd1[t] = rd1[(o_xh[p] * 2 + slot // 4) * 4 + slot % 4, t]
    rd2[z] = pd1[...]
    d2_args = (8, z, lambda q: pd1, lambda q: rd2.at[q], along, d2, e2)
    send_all(*d2_args)
    for d in FAR_FIRST[4:] + (0,):
        scatter(d, 0)
    for d in FAR_FIRST + (0,):
        scatter(d, 1)

    def spread(d, w):
        return remote(pc2[w], za[w].at[d], s4.at[w, d], r4.at[w, d], along((z + d) % 8))

    def hand_over(d, w):
        return remote(za[w].at[d], xa[w].at[d], s4x.at[w, d], r4x.at[w, d], partner)

    def start_gather(w):
        for d in FAR_FIRST:
            deal(d, w).wait_recv()
        piece = rc2[w][(z + 8 - jnp.where(z < 4, o_z[0], o_z[1])) % 8]
        pc2[w][...] = piece
        za[w][0] = piece
        for d in FAR_FIRST:
            spread(d, w).start()
        hand_over(0, w).start()

    start_gather(0)
    recv_all(*d2_args)
    for t, (p, n) in enumerate(lead):
        diag[k, me_plane, t] = rd2[o_z[p], t]
    d3_args = (16, me_plane, lambda q: diag.at[k, me_plane], lambda q: diag.at[k, q], plane, d3, e3)
    send_all(*d3_args)
    start_gather(1)

    def join(src, dst, i, w):
        return remote(src[w], dst[w], s5.at[i, w], r5.at[i, w], sib)

    for d in FAR_FIRST:
        spread(d, 0).wait_recv()
        hand_over(d, 0).start()
    join(za, zb, 0, 0).start()
    recv_all(*d3_args)
    remote(diag.at[k], diag.at[k], d4, e4, sib).start()
    for d in FAR_FIRST:
        spread(d, 1).wait_recv()
        hand_over(d, 1).start()
    join(za, zb, 0, 1).start()
    joined_lead = remote(diag.at[k], diag.at[1 - k], d4, e4, sib)
    joined_lead.wait_recv()

    rid = lax.broadcasted_iota(jnp.int32, (W, W), 0)
    cid = lax.broadcasted_iota(jnp.int32, (W, W), 1)
    eye = jnp.where(rid == cid, 1.0, 0.0).astype(F32)
    place_lead(diag, 0, wa)
    wb[...] = eye
    factor(wa, wb, 0, 6)

    def crossed(w):
        for d in range(8):
            hand_over(d, w).wait_recv()
        join(xa, xb, 1, w).start()

    def c1_args(w):
        return 8, me_row, lambda q: cst[w].at[q], lambda q: rc3[w].at[q], row_of, s6.at[w], r6.at[w]

    def c2_args(w):
        return 8, me_row, lambda q: pc3[w], lambda q: cbuf[w].at[q], row_of, s7.at[w], r7.at[w]

    def start_columns(w):
        join(za, zb, 0, w).wait_recv()
        join(xa, xb, 1, w).wait_recv()
        for p in range(2):
            for l in range(2):
                i = slots[l] % 8
                d = (z + 8 - 4 * p - i % 4) % 8
                mine = i // 4 == k
                cst[w][4 * p + 2 * l + xh] = jnp.where(mine, za[w][d], zb[w][d])
                cst[w][4 * p + 2 * l + 1 - xh] = jnp.where(mine, xa[w][d], xb[w][d])
        rc3[w][me_row] = cst[w][me_row]
        send_all(*c1_args(w))

    def pass_columns(w):
        recv_all(*c1_args(w))
        piece = rc3[w][jnp.where((me_row // 2) % 2 == 0, slots[0] // 8, slots[1] // 8)]
        pc3[w][...] = piece
        cbuf[w][me_row] = piece
        send_all(*c2_args(w))

    crossed(0)
    factor(wa, wb, 6, 9)
    crossed(1)
    start_columns(0)
    factor(wa, wb, 9, 12)
    start_columns(1)
    factor(wa, wb, 12, 16)
    low[0] = jnp.where(rid <= cid, wa[...], 0.0).T
    inv0 = wb[...]
    inv[0] = inv0
    place_lead(diag, 1, tile_a)
    f01 = nt(tile_a[...], inv0)
    f01_out[...] = f01
    place_lead(diag, 2, wa)
    wa[...] = wa[...] - nt(f01, f01)
    wb[...] = eye
    factor(wa, wb, 0, 7)
    pass_columns(0)
    pass_columns(1)
    factor(wa, wb, 7, 16)
    low[1] = jnp.where(rid <= cid, wa[...], 0.0).T
    inv[1] = wb[...]

    for d in range(8):
        t = (z + 8 - d) % 8
        for w in waves:
            for core, pieces in ((k, (za, xa)), (1 - k, (zb, xb))):
                rows[t // 4, 4 * core + t % 4, pl.ds(64 * xh + 32 * w, 32), :] = pieces[0][w][d]
                rows[t // 4, 4 * core + t % 4, pl.ds(64 * (1 - xh) + 32 * w, 32), :] = pieces[1][w][d]

    def mask(value, keeps):
        return jnp.concatenate(
            [jnp.where(keep, value[W * i : W * i + W], 0.0) for i, keep in enumerate(keeps)], axis=0
        )

    f0[...] = mask(nt3(rows[0].reshape(8 * W, W), inv[0]), keep_row[0])
    fh[:, :W], fl[:, :W] = parts(f0[...])
    f1 = mask(nt3(rows[1].reshape(8 * W, W) - nt3(f0[...], f01_out[...]), inv[1]), keep_row[1])
    fh[:, W:], fl[:, W:] = parts(f1)
    for l in range(2):
        first = col_node[l] == 0
        second = col_node[l] == 1
        for s in range(8):
            rows_s = slice(W * s, W * s + W)
            here = ((first & keep_row[0][s]), (second & keep_row[1][s]))
            edge = ((first & (row_node[s] == 0)), (second & (row_node[s] == 1)))
            tile = mat[l, s]
            tile = jnp.where(here[0], f0[rows_s], tile)
            tile = jnp.where(here[1], f1[rows_s], tile)
            tile = jnp.where(edge[0], low[0], tile)
            base[l, s] = jnp.where(edge[1], low[1], tile)
            fixed = here[0] | here[1] | edge[0] | edge[1]
            change = (row_node[s] >= col_node[l]) & jnp.logical_not(fixed)
            i = 8 * l + s
            info[i : i + 1, :] = jnp.where(change, jnp.ones((1, W), F32), 0.0)
    for p in range(2):
        for l in range(2):
            i = 16 + 2 * p + l
            info[i : i + 1, :] = jnp.where(pat[p, col_node[l]] == 1, jnp.ones((1, W), F32), 0.0)
    info[20:, :] = jnp.zeros((4, W), F32)
    for arguments in (d1_args, d2_args, d3_args, c1_args(0), c1_args(1), c2_args(0), c2_args(1)):
        sent_all(*arguments)
    for w in waves:
        for d in range(8):
            cross(d, w).wait_send()
            hand_over(d, w).wait_send()
            if d:
                deal(d, w).wait_send()
                spread(d, w).wait_send()
        join(za, zb, 0, w).wait_send()
        join(xa, xb, 1, w).wait_send()
    for copy in (split_lead, split_half, joined_lead):
        copy.wait_send()
    for w in waves:
        recv_all(*c2_args(w))
        for q in range(8):
            cols[q, 32 * w : 32 * w + 32, :] = cbuf[w][q]


def gather_tiles(mat, co, ro, pat):
    vmem = pl.BlockSpec(memory_space=pltpu.VMEM)
    hbm = pl.BlockSpec(memory_space=pltpu.HBM)
    dma = pltpu.SemaphoreType.DMA
    vm = lambda *shape: pltpu.VMEM(shape, F32)
    pair = lambda n: [dma((n,)), dma((n,))]
    pairs = lambda n: [dma((2, n)), dma((2, n))]
    out = lambda *shape, dtype=F32: jax.ShapeDtypeStruct(shape, dtype)
    return pl.pallas_call(
        comm_kernel,
        out_shape=(
            out(2, 8, W, W),
            out(8 * W, 2 * W, dtype=jnp.bfloat16),
            out(8 * W, 2 * W, dtype=jnp.bfloat16),
            out(2, W, W),
            out(W, W),
            out(8, 64, W),
            out(24, W),
        ),
        in_specs=[hbm] * 4,
        out_specs=(vmem,) * 7,
        scratch_shapes=[
            vm(2, 8, W, W),
            pltpu.SMEM((NODES,), jnp.int32),
            pltpu.SMEM((NODES,), jnp.int32),
            pltpu.SMEM((2, NODES), jnp.int32),
            vm(2, 4, W, W), vm(2, 4, W, W),
            vm(3, 64, W), vm(3, 64, W),
            vm(8, W, W), vm(3, 64, W), vm(2, 8, W, W),
            *[vm(8, 32, W)] * 6, *[vm(32, W)] * 2, *[vm(8, 32, W)] * 8,
            *[vm(8, 32, W)] * 4, *[vm(32, W)] * 2, *[vm(8, 32, W)] * 2,
            vm(16, 3, 4, W), vm(16, 3, 4, W), vm(3, 4, W), vm(8, 3, 4, W), vm(2, 16, 3, 4, W),
            vm(W, W), vm(W, W), vm(W, W), vm(2, W, W), vm(8 * W, W),
            dma((4,)),
            *pair(2), *pairs(8), *pairs(8), *pairs(8), *pairs(8), *pairs(2), *pairs(8), *pairs(8),
            *pair(16), *pair(8), *pair(16), dma, dma,
        ],
        compiler_params=pltpu.CompilerParams(
            collective_id=0, has_side_effects=True, vmem_limit_bytes=40 * 1024 * 1024
        ),
        name="gather_tiles",
    )(mat, co, ro, pat)


def lanes(x):
    return jnp.broadcast_to(x, (x.shape[0], W))


def subs(x):
    return jnp.broadcast_to(x, (8, W))


def factor(wa_ref, wb_ref, first, last):
    rid = lax.broadcasted_iota(jnp.int32, (8, W), 0)
    for c in range(8 * first, 8 * last, 8):
        wa = wa_ref[c : c + 8, :]
        wb = wb_ref[c : c + 8, :]
        cl = [lanes(wa[:, c + i : c + i + 1]) for i in range(8)]
        pa, pb, sc, lt = [], [], [], []
        for i in range(8):
            s = lax.rsqrt(subs(cl[i][i : i + 1]))
            li = cl[i] * s
            ra = subs(wa[i : i + 1]) * s
            rb = subs(wb[i : i + 1]) * s
            low = jnp.where(rid > i, li, 0.0)
            wa = jnp.where(rid == i, ra, wa - low * ra)
            wb = jnp.where(rid == i, rb, wb - low * rb)
            row = {}
            for j in range(i + 1, 8):
                row[j] = subs(li[j : j + 1])
                cl[j] = cl[j] - li * row[j]
            pa.append(ra)
            pb.append(rb)
            sc.append(s)
            lt.append(row)
        wa_ref[c : c + 8, :] = wa
        wb_ref[c : c + 8, :] = wb
        g = c + 8
        while g < W:
            size = min(16, W - g)
            tile = lambda v: jnp.concatenate([v] * (size // 8), axis=0) if size > 8 else v
            ga = wa_ref[g : g + size, :]
            gb = wb_ref[g : g + size, :]
            gc = [lanes(ga[:, c + i : c + i + 1]) for i in range(8)]
            for i in range(8):
                li = gc[i] * tile(sc[i])
                ga = ga - li * tile(pa[i])
                gb = gb - li * tile(pb[i])
                for j in range(i + 1, 8):
                    gc[j] = gc[j] - li * tile(lt[i][j])
            wa_ref[g : g + size, :] = ga
            wb_ref[g : g + size, :] = gb
            g += size


def nt(a, b):
    return lax.dot_general(a, b, (((1,), (1,)), ((), ())), precision=PRECISE, preferred_element_type=F32)


def nt16(a, b):
    return lax.dot_general(a, b, (((1,), (1,)), ((), ())), preferred_element_type=F32)


def parts(a):
    high = a.astype(jnp.bfloat16)
    return high, (a - high.astype(F32)).astype(jnp.bfloat16)


def nt3(a, b):
    ah, al = parts(a)
    bh, bl = parts(b)
    both = nt16(jnp.concatenate([ah, al], axis=1), jnp.concatenate([bh, bh], axis=1))
    return both + nt16(ah, bl)


def apply_kernel(base, fh, fl, inv, f01, cols, info, out, buf, sem):
    def flag(i):
        return info[i : i + 1, :] > 0.5

    def mask(value, p):
        return jnp.concatenate(
            [jnp.where(flag(16 + 2 * p + l), value[W * l : W * l + W], 0.0) for l in range(2)], axis=0
        )

    raw = lambda p: cols[4 * p : 4 * p + 4].reshape(2 * W, W)
    g0 = mask(nt3(raw(0), inv[0]), 0)
    g1 = mask(nt3(raw(1) - nt3(g0, f01[...]), inv[1]), 1)
    g0h, g0l = parts(g0)
    g1h, g1l = parts(g1)
    gh = jnp.concatenate([g0h, g1h], axis=1)
    gl = jnp.concatenate([g0l, g1l], axis=1)
    copies = []
    for s in range(0, 8, 4):
        both = slice(W * s, W * s + 4 * W)
        step = nt16(fh[both], gh) + nt16(fl[both], gh) + nt16(fh[both], gl)
        for l in range(2):
            for i in range(4):
                old = base[l, s + i]
                new = old - step[W * i : W * i + W, W * l : W * l + W]
                buf[l, s + i] = jnp.where(flag(8 * l + s + i), new, old)
            copy = pltpu.make_async_copy(buf.at[l, pl.ds(s, 4)], out.at[l, pl.ds(s, 4)], sem.at[l + s])
            copy.start()
            copies.append(copy)
    for copy in copies:
        copy.wait()


def apply_panels(base, fh, fl, inv, f01, cols, info):
    vmem = pl.BlockSpec(memory_space=pltpu.VMEM)
    return pl.pallas_call(
        apply_kernel,
        out_shape=jax.ShapeDtypeStruct((2, 8, W, W), F32),
        in_specs=[vmem] * 7,
        out_specs=pl.BlockSpec(memory_space=pltpu.HBM),
        scratch_shapes=[pltpu.VMEM((2, 8, W, W), F32), pltpu.SemaphoreType.DMA((8,))],
        compiler_params=pltpu.CompilerParams(vmem_limit_bytes=16 * 1024 * 1024),
        name="apply_panels",
    )(base, fh, fl, inv, f01, cols, info)


def body(matrix, col_owner, row_owner, pattern):
    held = [pltpu.with_memory_space_constraint(x, pltpu.HBM) for x in (matrix, col_owner, row_owner, pattern)]
    return apply_panels(*gather_tiles(*held))


def solution(mesh):
    return jax.shard_map(
        body,
        mesh=mesh,
        in_specs=(P("col", "row", None, None), P(), P(), P()),
        out_specs=P("col", "row", None, None),
        check_vma=False,
    )
```
